512 devices in a mesh: node: 8 (over y_hi, core), slab: 64 (over y_lo, x, z).
Axes of the slice: x: 4, y: 8 (y_hi: 4, y_lo: 2; y = y_hi * 2 + y_lo), z: 8, core: 2. Of those that a mesh axis runs over, the one named last changes fastest.
Arguments:
- adjoint_source: float32 [8, 6, 256, 64, 256], P('node', None, 'slab'), may hold values from -6 to 6
- stencil_coef: float32 [8, 4, 256, 64, 256], P('node', None, 'slab'), may hold values from 0.05 to 0.5
- flux_block: float32 [8, 6, 6], P('node'), may hold values from -1.25 to 1.25
- shape_metric: float32 [8, 6, 256, 64, 256], P('node', None, 'slab'), may hold values from -0.3125 to 0.3125
- wall_force: float32 [8, 256, 256], P('node', 'slab'), may hold values from -8 to 8
Outputs:
- wall_gradient: float32 [256, 256], P('slab', 'node')
The draws below stay inside these ranges and needn't reach their ends.
All inputs are finite; a program needn't handle non-finite values.
Results may differ from the reference program's by a relative error of at most 0.00014.
Values sent between devices are 32-bit elements; how exact they have to be, the bound alone decides.
A program may use at most 64 MiB of HBM per device.

```python
import math
import jax
import jax.numpy as jnp
from jax import lax

NV = 6
NY = 64
NZ = 256
ITERS = 3
NODES = 8
NX = 256


def draw_wall_force(key, part):
    offset = jax.random.uniform(jax.random.fold_in(key, 11), (NODES, 1, 1), jnp.float32, -2.0, 2.0)
    noise = jnp.clip(jax.random.normal(jax.random.fold_in(key, 12), (NODES, NX, NZ), jnp.float32), -5.0, 5.0)
    return offset + noise


def block_scale(key, shape, shards, low, high):
    gain, own = 1.0, jax.random.fold_in(key, 6)
    for dim, blocks in shards:
        heights = jnp.exp(jax.random.uniform(jax.random.fold_in(own, dim), (blocks,), jnp.float32, low / len(shards), high / len(shards)))
        gain = gain * jnp.repeat(heights, shape[dim] // blocks).reshape([-1 if axis == dim else 1 for axis in range(len(shape))])
    return gain


def bell_draw(key, shape, scale, reach, pieces=(), held_as=jnp.bfloat16):
    factor_of = block_scale(key, shape, pieces, -0.22, 0.18) if pieces else 1.0
    values = jax.random.normal(key, shape, jnp.float32) * scale * factor_of
    return jnp.minimum(jnp.maximum(values, -reach), reach).astype(held_as)


def setup_inputs(seed: int = 0) -> dict:
    key_list = jax.random.split(jax.random.key(seed), 6)
    return {
        "adjoint_source": bell_draw(key_list[0], (NODES, NV, NX, NY, NZ), 1.0, 6.0, ((0, 8), (2, 64)), jnp.float32),
        "stencil_coef": jnp.clip(jnp.exp(math.log(0.5) - 2.3025851 * jax.random.uniform(key_list[1], (NODES, 4, NX, NY, NZ), jnp.float32) ** block_scale(key_list[1], (NODES, 4, NX, NY, NZ), ((0, 8), (2, 64)), -0.2, 0.2)), 0.05, 0.5),
        "flux_block": bell_draw(key_list[2], (NODES, NV, NV), (4 * NV) ** -0.5, 1.25, ((0, 8),), jnp.float32),
        "shape_metric": bell_draw(key_list[3], (NODES, NV, NX, NY, NZ), (NV * NY) ** -0.5, 0.3125, ((0, 8), (2, 64)), jnp.float32),
        "wall_force": draw_wall_force(jax.random.fold_in(key_list[5], 71), 0),
    }


def sweep(psi, source, coef, diag, block):
    padded = jnp.pad(psi, ((0, 0), (1, 1), (1, 1), (1, 1)))
    middle = padded[:, 1:-1, 1:-1, 1:-1]
    coupled = coef[1] * (padded[:, 2:, 1:-1, 1:-1] + padded[:, :-2, 1:-1, 1:-1])
    coupled = coupled + coef[2] * (padded[:, 1:-1, 2:, 1:-1] + padded[:, 1:-1, :-2, 1:-1])
    coupled = coupled + coef[3] * (padded[:, 1:-1, 1:-1, 2:] + padded[:, 1:-1, 1:-1, :-2])
    mixed = jnp.einsum('vw,vxyz->wxyz', block, coupled, precision=lax.Precision.HIGHEST)
    return middle + (source - (diag * middle - mixed)) / diag

def reference(adjoint_source, stencil_coef, flux_block, shape_metric, wall_force):
    sens_list = []
    objective_list = []
    for node_id in range(NODES):
        source = adjoint_source[node_id]
        coef = stencil_coef[node_id]
        diag = 0.5 + coef[0] + 2.4 * (coef[1] + coef[2] + coef[3])
        psi = source / diag
        for step in range(ITERS - 1):
            psi = sweep(psi, source, coef, diag, flux_block[node_id])
        sens_list.append(lax.optimization_barrier(jnp.sum(psi * shape_metric[node_id], axis=(0, 2))))
        objective_list.append(jnp.mean(wall_force[node_id]))
    objective = jnp.stack(objective_list)
    order = jnp.arange(NODES, dtype=jnp.float32)
    weight = jnp.sin(math.pi * (order + 0.5) / NODES)
    weight = weight / jnp.sum(weight)
    mean_value = jnp.sum(weight * objective)
    variance = jnp.sum(weight * (objective - mean_value) ** 2)
    spread = jnp.sqrt(variance + 0.25)
    factor = weight * (1.0 + 2.0 * (objective - mean_value) / spread)
    total = jnp.zeros_like(sens_list[0])
    for node_id in range(NODES):
        total = total + factor[node_id] * sens_list[node_id]
    return total
```

```python
import functools
import math

import jax
import jax.numpy as jnp
from jax import lax
from jax.experimental import pallas as pl
from jax.experimental.pallas import tpu as pltpu
from jax.sharding import PartitionSpec as P

MESH = pl.DeviceIdType.MESH
CHUNKS = 2
ROWS = 16
LANES = 128


def shifted_pairs(p):
    ny, nz = p.shape
    row = lax.broadcasted_iota(jnp.int32, p.shape, 0)
    lane = lax.broadcasted_iota(jnp.int32, p.shape, 1)
    above = jnp.where(row == 0, 0.0, pltpu.roll(p, 1, 0))
    below = jnp.where(row == ny - 1, 0.0, pltpu.roll(p, ny - 1, 0))
    before = jnp.where(lane == 0, 0.0, pltpu.roll(p, 1, 1))
    after = jnp.where(lane == nz - 1, 0.0, pltpu.roll(p, nz - 1, 1))
    return above + below, before + after


def fold_rows(block):
    return jnp.sum(jnp.reshape(block, (block.shape[0] // 8, 8, block.shape[1])), axis=0)


def kernel(
    nodes, slabs, inner, cells,
    source, coef, flux, shape, wall, out,
    psi0, cf, psi1, mix, tv, halo0, halo1, acc, wallv, obj, objn, own, sens, fin,
    load_sem, send0, recv0, send1, recv1, obj_send, obj_recv, fin_send, fin_recv,
):
    me, nd = lax.axis_index("slab"), lax.axis_index("node")
    outer = slabs // inner
    place, group = lax.rem(me, inner), lax.div(me, inner)
    right, left = lax.rem(me + 1, slabs), lax.rem(me + slabs - 1, slabs)
    nv, nx, ny, nz = psi0.shape
    part = ny // CHUNKS

    peers = [
        [{"slab": group * inner + lax.rem(place + d, inner)} for d in range(1, inner)],
        [{"slab": lax.rem(group + d, outer) * inner + place} for d in range(1, outer)],
        [{"node": lax.rem(nd + d, nodes)} for d in range(1, nodes)],
    ]

    barrier = pltpu.get_barrier_semaphore()
    everyone = [{"slab": left}, {"slab": right}] + peers[0] + peers[1] + peers[2]
    for peer in everyone:
        pl.semaphore_signal(barrier, inc=1, device_id=peer, device_id_type=MESH)

    loads = {}

    def load(name, src, dst, index):
        loads[name] = pltpu.make_async_copy(src, dst, load_sem.at[index])
        loads[name].start()

    load("wall", wall.at[0], wallv, 0)
    order = [0, nx - 1] + list(range(1, nx - 1))
    for i, x in enumerate(order):
        load(("coef", x), coef.at[0, :, x], cf.at[:, x], 1 + 2 * i)
        load(("source", x), source.at[0, :, x], psi0.at[:, x], 2 + 2 * i)
    load("shape", shape.at[0], tv, 1 + 2 * nx)

    started = []

    def remote(src, dst, send, recv, peer):
        copy = pltpu.make_async_remote_copy(
            src_ref=src, dst_ref=dst, send_sem=send, recv_sem=recv,
            device_id=peer, device_id_type=MESH,
        )
        copy.start()
        started.append(copy)
        return copy

    def spread(stage, slot):
        copies = []
        for d, peer in enumerate(peers[stage]):
            dst = objn.at[nd] if stage == 2 else obj.at[stage, d]
            copies.append(
                remote(own.at[stage], dst, obj_send.at[stage, d], obj_recv.at[stage, d], peer)
            )
        return copies

    def collect(stage, copies):
        total = own[stage]
        for d, copy in enumerate(copies):
            copy.wait_recv()
            total = total + obj[stage, d]
        return total

    loads["wall"].wait()
    w = wallv[...]
    width = w.shape[1]
    lane_sum = w[:, 0:LANES]
    for k in range(LANES, width, LANES):
        lane_sum = lane_sum + w[:, k:k + LANES]
    own[0] = jnp.sum(lane_sum, axis=0, keepdims=True)

    def start_psi(x, first, count):
        def step(i, carry):
            rows = pl.ds(pl.multiple_of(first + i * 8, 8), 8)
            c1, c2, c3 = cf[1, x, rows, :], cf[2, x, rows, :], cf[3, x, rows, :]
            inverse = 1.0 / (0.5 + cf[0, x, rows, :] + 2.4 * (c1 + c2 + c3))
            cf[1, x, rows, :] = c1 * inverse
            cf[2, x, rows, :] = c2 * inverse
            cf[3, x, rows, :] = c3 * inverse
            for v in range(nv):
                psi0[v, x, rows, :] = psi0[v, x, rows, :] * inverse
            return carry
        lax.fori_loop(0, count // 8, step, 0)

    def send_plane(field, halo, side, c, send, recv):
        x, peer = (nx - 1, right) if side == 0 else (0, left)
        rows = pl.ds(c * part, part)
        return remote(
            field.at[:, x, rows, :], halo.at[side, :, rows, :],
            send.at[side, c], recv.at[side, c], {"slab": peer},
        )

    pl.semaphore_wait(barrier, len(everyone))
    stage_a = spread(0, place)
    halo_copies = {}
    for x in (0, nx - 1):
        loads[("coef", x)].wait()
        loads[("source", x)].wait()
    for c in range(CHUNKS):
        for x, side in ((0, 1), (nx - 1, 0)):
            start_psi(x, c * part, part)
            halo_copies[side, c] = send_plane(psi0, halo0, side, c, send0, recv0)
    for x in range(1, nx - 1):
        loads[("coef", x)].wait()
        loads[("source", x)].wait()
        start_psi(x, 0, ny)

    own[1] = collect(0, stage_a)
    stage_b = spread(1, group)

    def stencil(field, x, v):
        p = field[v, x]
        beside_y, beside_z = shifted_pairs(p)
        if x == 0:
            beside_x = field[v, 1]
        elif x == nx - 1:
            beside_x = field[v, nx - 2]
        else:
            beside_x = field[v, x - 1] + field[v, x + 1]
        return cf[1, x] * beside_x + cf[2, x] * beside_y + cf[3, x] * beside_z

    def first_sweep(x):
        def couple(v, carry):
            mix[v] = stencil(psi0, x, v)
            return carry
        lax.fori_loop(0, nv, couple, 0)

        def combine(i, carry):
            rows = pl.ds(pl.multiple_of(i * ROWS, ROWS), ROWS)
            held = [mix[v, rows, :] for v in range(nv)]
            for o in range(nv):
                total = psi0[o, x, rows, :]
                for v in range(nv):
                    total = total + flux[0, v, o] * held[v]
                psi1[o, x, rows, :] = total
            return carry
        lax.fori_loop(0, ny // ROWS, combine, 0)

    for x in order:
        first_sweep(x)

    own[2] = collect(1, stage_b)
    objn[nd] = own[2]
    stage_c = spread(2, nd)

    has = (
        jnp.where(me > 0, 1.0, 0.0).astype(jnp.float32),
        jnp.where(me < slabs - 1, 1.0, 0.0).astype(jnp.float32),
    )
    later_copies = {}
    for c in range(CHUNKS):
        for side in (1, 0):
            came = 0 if side == 1 else 1
            x = 0 if side == 1 else nx - 1
            halo_copies[came, c].wait_recv()

            def join(i, carry):
                rows = pl.ds(pl.multiple_of(c * part + i * ROWS, ROWS), ROWS)
                held = [halo0[came, v, rows, :] for v in range(nv)]
                a = cf[1, x, rows, :] * has[came]
                for o in range(nv):
                    total = flux[0, 0, o] * held[0]
                    for v in range(1, nv):
                        total = total + flux[0, v, o] * held[v]
                    psi1[o, x, rows, :] = psi1[o, x, rows, :] + a * total
                return carry
            lax.fori_loop(0, part // ROWS, join, 0)
            later_copies[side, c] = send_plane(psi1, halo1, side, c, send1, recv1)

    loads["shape"].wait()
    for x in range(nx):
        def adjoint(i, total_sum):
            rows = pl.ds(pl.multiple_of(i * ROWS, ROWS), ROWS)
            held = [tv[v, x, rows, :] for v in range(nv)]
            product = held[0] * psi0[0, x, rows, :]
            for v in range(1, nv):
                product = product + held[v] * psi0[v, x, rows, :]
            for v in range(nv):
                total = flux[0, v, 0] * held[0]
                for o in range(1, nv):
                    total = total + flux[0, v, o] * held[o]
                tv[v, x, rows, :] = total
            return total_sum + fold_rows(product)
        acc[x] = lax.fori_loop(0, ny // ROWS, adjoint, jnp.zeros((8, nz), jnp.float32))

    for x in range(nx):
        def last_sweep(v, total):
            return total + fold_rows(tv[v, x] * stencil(psi1, x, v))
        acc[x] = lax.fori_loop(0, nv, last_sweep, acc[x])

    for copy in stage_c:
        copy.wait_recv()
    rows_of = lax.broadcasted_iota(jnp.int32, (nodes, LANES), 0)
    raw = [math.sin(math.pi * (n + 0.5) / nodes) for n in range(nodes)]
    weight = jnp.zeros((nodes, LANES), jnp.float32)
    for n in range(nodes):
        weight = jnp.where(rows_of == n, raw[n] / sum(raw), weight)
    lane_parts = jnp.zeros((nodes, LANES), jnp.float32)
    for n in range(nodes):
        lane_parts = jnp.where(rows_of == n, objn[n], lane_parts)
    objective = jnp.sum(lane_parts, axis=1, keepdims=True) * (1.0 / cells)
    mean_value = jnp.sum(weight * objective, axis=0, keepdims=True)
    variance = jnp.sum(weight * (objective - mean_value) ** 2, axis=0, keepdims=True)
    factor = weight * (1.0 + 2.0 * (objective - mean_value) / jnp.sqrt(variance + 0.25))

    for c in range(CHUNKS):
        for side in (1, 0):
            came = 0 if side == 1 else 1
            x = 0 if side == 1 else nx - 1
            later_copies[came, c].wait_recv()

            def take(i, total):
                rows = pl.ds(pl.multiple_of(c * part + i * ROWS, ROWS), ROWS)
                product = tv[0, x, rows, :] * halo1[came, 0, rows, :]
                for v in range(1, nv):
                    product = product + tv[v, x, rows, :] * halo1[came, v, rows, :]
                return total + fold_rows(cf[1, x, rows, :] * has[came] * product)
            acc[x] = lax.fori_loop(0, part // ROWS, take, acc[x])

    for x in range(nx):
        line = jnp.sum(acc[x], axis=0, keepdims=True)
        for k in range(nz // LANES):
            sens[k, x:x + 1, :] = line[:, k * LANES:(k + 1) * LANES]

    width = nz // nodes
    per_tile = LANES // width
    finals = []
    for d, peer in enumerate(peers[2]):
        finals.append(
            remote(
                sens.at[lax.div(peer["node"], per_tile)], fin.at[nd],
                fin_send.at[d], fin_recv.at[d], peer,
            )
        )
    fin[nd] = sens[lax.div(nd, per_tile)]
    for copy in finals:
        copy.wait_recv()
    total = factor[0:1, :] * fin[0]
    for n in range(1, nodes):
        total = total + factor[n:n + 1, :] * fin[n]
    column = lax.rem(nd, per_tile)
    result = total[:, 0:width]
    for k in range(1, per_tile):
        result = jnp.where(column == k, total[:, k * width:(k + 1) * width], result)
    out[...] = result
    for copy in started:
        copy.wait_send()


def solution(mesh):
    nodes, slabs = mesh.shape["node"], mesh.shape["slab"]
    inner = 2 ** (int(math.log2(slabs)) // 2)

    def per_device(source, coef, flux, shape, wall):
        _, nv, nx, ny, nz = source.shape
        f32 = jnp.float32
        dma = pltpu.SemaphoreType.DMA
        hbm = pl.BlockSpec(memory_space=pltpu.HBM)
        most = max(inner, slabs // inner, nodes) - 1
        return pl.pallas_call(
            functools.partial(kernel, nodes, slabs, inner, nx * slabs * nz),
            out_shape=jax.ShapeDtypeStruct((nx, nz // nodes), f32),
            in_specs=[hbm, hbm, pl.BlockSpec(memory_space=pltpu.SMEM), hbm, hbm],
            out_specs=pl.BlockSpec(memory_space=pltpu.VMEM),
            scratch_shapes=[
                pltpu.VMEM((nv, nx, ny, nz), f32),
                pltpu.VMEM((4, nx, ny, nz), f32),
                pltpu.VMEM((nv, nx, ny, nz), f32),
                pltpu.VMEM((nv, ny, nz), f32),
                pltpu.VMEM((nv, nx, ny, nz), f32),
                pltpu.VMEM((2, nv, ny, nz), f32),
                pltpu.VMEM((2, nv, ny, nz), f32),
                pltpu.VMEM((nx, 8, nz), f32),
                pltpu.VMEM((nx, nz), f32),
                pltpu.VMEM((2, most, 1, LANES), f32),
                pltpu.VMEM((nodes, 1, LANES), f32),
                pltpu.VMEM((3, 1, LANES), f32),
                pltpu.VMEM((nz // LANES, nx, LANES), f32),
                pltpu.VMEM((nodes, nx, LANES), f32),
                dma((2 + 2 * nx,)),
                dma((2, CHUNKS)),
                dma((2, CHUNKS)),
                dma((2, CHUNKS)),
                dma((2, CHUNKS)),
                dma((3, most)),
                dma((3, most)),
                dma((nodes - 1,)),
                dma((nodes - 1,)),
            ],
            compiler_params=pltpu.CompilerParams(
                collective_id=0, has_side_effects=True, vmem_limit_bytes=32 * 2 ** 20
            ),
        )(source, coef, flux, shape, wall)

    return jax.shard_map(
        per_device,
        mesh=mesh,
        in_specs=(
            P("node", None, "slab", None, None),
            P("node", None, "slab", None, None),
            P("node", None, None),
            P("node", None, "slab", None, None),
            P("node", "slab", None),
        ),
        out_specs=P("slab", "node"),
        check_vma=False,
    )
```

```python
import functools
import math

import jax
import jax.numpy as jnp
from jax import lax
from jax.experimental import pallas as pl
from jax.experimental.pallas import tpu as pltpu
from jax.sharding import PartitionSpec as P

MESH = pl.DeviceIdType.MESH
CHUNKS = 2
ROWS = 16
LANES = 128


def shifted_pairs(p):
    ny, nz = p.shape
    row = lax.broadcasted_iota(jnp.int32, p.shape, 0)
    lane = lax.broadcasted_iota(jnp.int32, p.shape, 1)
    above = jnp.where(row == 0, 0.0, pltpu.roll(p, 1, 0))
    below = jnp.where(row == ny - 1, 0.0, pltpu.roll(p, ny - 1, 0))
    before = jnp.where(lane == 0, 0.0, pltpu.roll(p, 1, 1))
    after = jnp.where(lane == nz - 1, 0.0, pltpu.roll(p, nz - 1, 1))
    return above + below, before + after


def fold_rows(block):
    return jnp.sum(jnp.reshape(block, (block.shape[0] // 8, 8, block.shape[1])), axis=0)


def kernel(
    nodes, slabs, inner, cells,
    source, coef, flux_in, shape, wall, out,
    flux, psi0, cf, psi1, mix, tv, halo0, halo1, acc, wallv, obj, objn, own, sens, fin,
    load_sem, send0, recv0, send1, recv1, obj_send, obj_recv, fin_send, fin_recv,
):
    me, nd = lax.axis_index("slab"), lax.axis_index("node")
    outer = slabs // inner
    place, group = lax.rem(me, inner), lax.div(me, inner)
    right, left = lax.rem(me + 1, slabs), lax.rem(me + slabs - 1, slabs)
    nv, nx, ny, nz = psi0.shape
    part = ny // CHUNKS

    peers = [
        [{"slab": group * inner + lax.rem(place + d, inner)} for d in range(1, inner)],
        [{"slab": lax.rem(group + d, outer) * inner + place} for d in range(1, outer)],
        [{"node": lax.rem(nd + d, nodes)} for d in range(1, nodes)],
    ]

    barrier = pltpu.get_barrier_semaphore()
    everyone = [{"slab": left}, {"slab": right}] + peers[0] + peers[1] + peers[2]
    for peer in everyone:
        pl.semaphore_signal(barrier, inc=1, device_id=peer, device_id_type=MESH)

    loads = {}

    def load(name, src, dst, index):
        loads[name] = pltpu.make_async_copy(src, dst, load_sem.at[index])
        loads[name].start()

    load("wall", wall.at[0], wallv, 0)
    order = [0, nx - 1] + list(range(1, nx - 1))
    for i, x in enumerate(order):
        load(("coef", x), coef.at[0, :, x], cf.at[:, x], 1 + 2 * i)
        load(("source", x), source.at[0, :, x], psi0.at[:, x], 2 + 2 * i)
    load("flux", flux_in, flux, 1 + 2 * nx)
    load("shape", shape.at[0], tv, 2 + 2 * nx)

    started = []

    def remote(src, dst, send, recv, peer):
        copy = pltpu.make_async_remote_copy(
            src_ref=src, dst_ref=dst, send_sem=send, recv_sem=recv,
            device_id=peer, device_id_type=MESH,
        )
        copy.start()
        started.append(copy)
        return copy

    def spread(stage, slot):
        copies = []
        for d, peer in enumerate(peers[stage]):
            dst = objn.at[nd] if stage == 2 else obj.at[stage, d]
            copies.append(
                remote(own.at[stage], dst, obj_send.at[stage, d], obj_recv.at[stage, d], peer)
            )
        return copies

    def collect(stage, copies):
        total = own[stage]
        for d, copy in enumerate(copies):
            copy.wait_recv()
            total = total + obj[stage, d]
        return total

    loads["wall"].wait()
    w = wallv[...]
    width = w.shape[1]
    lane_sum = w[:, 0:LANES]
    for k in range(LANES, width, LANES):
        lane_sum = lane_sum + w[:, k:k + LANES]
    own[0] = jnp.sum(lane_sum, axis=0, keepdims=True)

    def start_psi(x, first, count):
        def step(i, carry):
            rows = pl.ds(pl.multiple_of(first + i * 8, 8), 8)
            c1, c2, c3 = cf[1, x, rows, :], cf[2, x, rows, :], cf[3, x, rows, :]
            inverse = 1.0 / (0.5 + cf[0, x, rows, :] + 2.4 * (c1 + c2 + c3))
            cf[1, x, rows, :] = c1 * inverse
            cf[2, x, rows, :] = c2 * inverse
            cf[3, x, rows, :] = c3 * inverse
            for v in range(nv):
                psi0[v, x, rows, :] = psi0[v, x, rows, :] * inverse
            return carry
        lax.fori_loop(0, count // 8, step, 0)

    def send_plane(field, halo, side, c, send, recv):
        x, peer = (nx - 1, right) if side == 0 else (0, left)
        rows = pl.ds(c * part, part)
        return remote(
            field.at[:, x, rows, :], halo.at[side, :, rows, :],
            send.at[side, c], recv.at[side, c], {"slab": peer},
        )

    pl.semaphore_wait(barrier, len(everyone))
    stage_a = spread(0, place)
    halo_copies = {}
    for x in (0, nx - 1):
        loads[("coef", x)].wait()
        loads[("source", x)].wait()
    for c in range(CHUNKS):
        for x, side in ((0, 1), (nx - 1, 0)):
            start_psi(x, c * part, part)
            halo_copies[side, c] = send_plane(psi0, halo0, side, c, send0, recv0)
    for x in range(1, nx - 1):
        loads[("coef", x)].wait()
        loads[("source", x)].wait()
        start_psi(x, 0, ny)

    own[1] = collect(0, stage_a)
    stage_b = spread(1, group)

    def stencil(field, x, v):
        p = field[v, x]
        beside_y, beside_z = shifted_pairs(p)
        if x == 0:
            beside_x = field[v, 1]
        elif x == nx - 1:
            beside_x = field[v, nx - 2]
        else:
            beside_x = field[v, x - 1] + field[v, x + 1]
        return cf[1, x] * beside_x + cf[2, x] * beside_y + cf[3, x] * beside_z

    def first_sweep(x):
        def couple(v, carry):
            mix[v] = stencil(psi0, x, v)
            return carry
        lax.fori_loop(0, nv, couple, 0)

        def combine(i, carry):
            rows = pl.ds(pl.multiple_of(i * ROWS, ROWS), ROWS)
            held = [mix[v, rows, :] for v in range(nv)]
            for o in range(nv):
                total = psi0[o, x, rows, :]
                for v in range(nv):
                    total = total + flux[v, 0, o] * held[v]
                psi1[o, x, rows, :] = total
            return carry
        lax.fori_loop(0, ny // ROWS, combine, 0)

    loads["flux"].wait()
    for x in order:
        first_sweep(x)

    own[2] = collect(1, stage_b)
    objn[nd] = own[2]
    stage_c = spread(2, nd)

    has = (
        jnp.where(me > 0, 1.0, 0.0).astype(jnp.float32),
        jnp.where(me < slabs - 1, 1.0, 0.0).astype(jnp.float32),
    )
    later_copies = {}
    for c in range(CHUNKS):
        for side in (1, 0):
            came = 0 if side == 1 else 1
            x = 0 if side == 1 else nx - 1
            halo_copies[came, c].wait_recv()

            def join(i, carry):
                rows = pl.ds(pl.multiple_of(c * part + i * ROWS, ROWS), ROWS)
                held = [halo0[came, v, rows, :] for v in range(nv)]
                a = cf[1, x, rows, :] * has[came]
                for o in range(nv):
                    total = flux[0, 0, o] * held[0]
                    for v in range(1, nv):
                        total = total + flux[v, 0, o] * held[v]
                    psi1[o, x, rows, :] = psi1[o, x, rows, :] + a * total
                return carry
            lax.fori_loop(0, part // ROWS, join, 0)
            later_copies[side, c] = send_plane(psi1, halo1, side, c, send1, recv1)

    loads["shape"].wait()
    for x in range(nx):
        def adjoint(i, total_sum):
            rows = pl.ds(pl.multiple_of(i * ROWS, ROWS), ROWS)
            held = [tv[v, x, rows, :] for v in range(nv)]
            product = held[0] * psi0[0, x, rows, :]
            for v in range(1, nv):
                product = product + held[v] * psi0[v, x, rows, :]
            for v in range(nv):
                total = flux[v, 0, 0] * held[0]
                for o in range(1, nv):
                    total = total + flux[v, 0, o] * held[o]
                tv[v, x, rows, :] = total
            return total_sum + fold_rows(product)
        acc[x] = lax.fori_loop(0, ny // ROWS, adjoint, jnp.zeros((8, nz), jnp.float32))

    for x in range(nx):
        def last_sweep(v, total):
            return total + fold_rows(tv[v, x] * stencil(psi1, x, v))
        acc[x] = lax.fori_loop(0, nv, last_sweep, acc[x])

    for copy in stage_c:
        copy.wait_recv()
    rows_of = lax.broadcasted_iota(jnp.int32, (nodes, LANES), 0)
    raw = [math.sin(math.pi * (n + 0.5) / nodes) for n in range(nodes)]
    weight = jnp.zeros((nodes, LANES), jnp.float32)
    for n in range(nodes):
        weight = jnp.where(rows_of == n, raw[n] / sum(raw), weight)
    lane_parts = jnp.zeros((nodes, LANES), jnp.float32)
    for n in range(nodes):
        lane_parts = jnp.where(rows_of == n, objn[n], lane_parts)
    objective = jnp.sum(lane_parts, axis=1, keepdims=True) * (1.0 / cells)
    mean_value = jnp.sum(weight * objective, axis=0, keepdims=True)
    variance = jnp.sum(weight * (objective - mean_value) ** 2, axis=0, keepdims=True)
    factor = weight * (1.0 + 2.0 * (objective - mean_value) / jnp.sqrt(variance + 0.25))

    for c in range(CHUNKS):
        for side in (1, 0):
            came = 0 if side == 1 else 1
            x = 0 if side == 1 else nx - 1
            later_copies[came, c].wait_recv()

            def take(i, total):
                rows = pl.ds(pl.multiple_of(c * part + i * ROWS, ROWS), ROWS)
                product = tv[0, x, rows, :] * halo1[came, 0, rows, :]
                for v in range(1, nv):
                    product = product + tv[v, x, rows, :] * halo1[came, v, rows, :]
                return total + fold_rows(cf[1, x, rows, :] * has[came] * product)
            acc[x] = lax.fori_loop(0, part // ROWS, take, acc[x])

    for x in range(nx):
        line = jnp.sum(acc[x], axis=0, keepdims=True)
        for k in range(nz // LANES):
            sens[k, x:x + 1, :] = line[:, k * LANES:(k + 1) * LANES]

    width = nz // nodes
    per_tile = LANES // width
    finals = []
    for d, peer in enumerate(peers[2]):
        finals.append(
            remote(
                sens.at[lax.div(peer["node"], per_tile)], fin.at[nd],
                fin_send.at[d], fin_recv.at[d], peer,
            )
        )
    fin[nd] = sens[lax.div(nd, per_tile)]
    for copy in finals:
        copy.wait_recv()
    total = factor[0:1, :] * fin[0]
    for n in range(1, nodes):
        total = total + factor[n:n + 1, :] * fin[n]
    column = lax.rem(nd, per_tile)
    result = total[:, 0:width]
    for k in range(1, per_tile):
        result = jnp.where(column == k, total[:, k * width:(k + 1) * width], result)
    out[...] = result
    for copy in started:
        copy.wait_send()


def solution(mesh):
    nodes, slabs = mesh.shape["node"], mesh.shape["slab"]
    inner = 2 ** (int(math.log2(slabs)) // 2)

    def per_device(source, coef, flux, shape, wall):
        _, nv, nx, ny, nz = source.shape
        f32 = jnp.float32
        dma = pltpu.SemaphoreType.DMA
        hbm = pl.BlockSpec(memory_space=pltpu.HBM)
        most = max(inner, slabs // inner, nodes) - 1
        return pl.pallas_call(
            functools.partial(kernel, nodes, slabs, inner, nx * slabs * nz),
            out_shape=jax.ShapeDtypeStruct((nx, nz // nodes), f32),
            in_specs=[hbm, hbm, hbm, hbm, hbm],
            out_specs=pl.BlockSpec(memory_space=pltpu.VMEM),
            scratch_shapes=[
                pltpu.SMEM((nv, 1, nv), f32),
                pltpu.VMEM((nv, nx, ny, nz), f32),
                pltpu.VMEM((4, nx, ny, nz), f32),
                pltpu.VMEM((nv, nx, ny, nz), f32),
                pltpu.VMEM((nv, ny, nz), f32),
                pltpu.VMEM((nv, nx, ny, nz), f32),
                pltpu.VMEM((2, nv, ny, nz), f32),
                pltpu.VMEM((2, nv, ny, nz), f32),
                pltpu.VMEM((nx, 8, nz), f32),
                pltpu.VMEM((nx, nz), f32),
                pltpu.VMEM((2, most, 1, LANES), f32),
                pltpu.VMEM((nodes, 1, LANES), f32),
                pltpu.VMEM((3, 1, LANES), f32),
                pltpu.VMEM((nz // LANES, nx, LANES), f32),
                pltpu.VMEM((nodes, nx, LANES), f32),
                dma((3 + 2 * nx,)),
                dma((2, CHUNKS)),
                dma((2, CHUNKS)),
                dma((2, CHUNKS)),
                dma((2, CHUNKS)),
                dma((3, most)),
                dma((3, most)),
                dma((nodes - 1,)),
                dma((nodes - 1,)),
            ],
            compiler_params=pltpu.CompilerParams(
                collective_id=0, has_side_effects=True, vmem_limit_bytes=60 * 2 ** 20
            ),
        )(source, coef, jnp.transpose(flux, (1, 0, 2)), shape, wall)

    return jax.shard_map(
        per_device,
        mesh=mesh,
        in_specs=(
            P("node", None, "slab", None, None),
            P("node", None, "slab", None, None),
            P("node", None, None),
            P("node", None, "slab", None, None),
            P("node", "slab", None),
        ),
        out_specs=P("slab", "node"),
        check_vma=False,
    )
```

```python
import functools
import math

import jax
import jax.numpy as jnp
from jax import lax
from jax.experimental import pallas as pl
from jax.experimental.pallas import tpu as pltpu
from jax.sharding import PartitionSpec as P

MESH = pl.DeviceIdType.MESH
CHUNKS = 4
ROWS = 16
LANES = 128


def shifted_pairs(p):
    ny, nz = p.shape
    row = lax.broadcasted_iota(jnp.int32, p.shape, 0)
    lane = lax.broadcasted_iota(jnp.int32, p.shape, 1)
    above = jnp.where(row == 0, 0.0, pltpu.roll(p, 1, 0))
    below = jnp.where(row == ny - 1, 0.0, pltpu.roll(p, ny - 1, 0))
    before = jnp.where(lane == 0, 0.0, pltpu.roll(p, 1, 1))
    after = jnp.where(lane == nz - 1, 0.0, pltpu.roll(p, nz - 1, 1))
    return above + below, before + after


def fold_rows(block):
    return jnp.sum(jnp.reshape(block, (block.shape[0] // 8, 8, block.shape[1])), axis=0)


def kernel(
    nodes, slabs, inner, cells,
    source, coef, flux_in, shape, wall, out,
    flux, psi0, cf, psi1, mix, tv, halo0, halo1, acc, wallv, obj, objn, own, sens, fin,
    load_sem, send0, recv0, send1, recv1, obj_send, obj_recv, fin_send, fin_recv,
):
    me, nd = lax.axis_index("slab"), lax.axis_index("node")
    outer = slabs // inner
    place, group = lax.rem(me, inner), lax.div(me, inner)
    has_left, has_right = me > 0, me < slabs - 1
    left, right = {"slab": me - 1}, {"slab": me + 1}
    nv, nx, ny, nz = psi0.shape
    part = ny // CHUNKS

    peers = [
        [{"slab": group * inner + lax.rem(place + d, inner)} for d in range(1, inner)],
        [{"slab": lax.rem(group + d, outer) * inner + place} for d in range(1, outer)],
        [{"node": lax.rem(nd + d, nodes)} for d in range(1, nodes)],
    ]

    barrier = pltpu.get_barrier_semaphore()

    def greet(peer):
        pl.semaphore_signal(barrier, inc=1, device_id=peer, device_id_type=MESH)

    pl.when(has_left & (place == 0))(lambda: greet(left))
    pl.when(has_right & (place == inner - 1))(lambda: greet(right))
    everyone = peers[0] + peers[1] + peers[2]
    for peer in everyone:
        greet(peer)
    beyond = jnp.where(has_left & (place == 0), 1, 0) + jnp.where(has_right & (place == inner - 1), 1, 0)

    loads = {}

    def load(name, src, dst, index):
        loads[name] = pltpu.make_async_copy(src, dst, load_sem.at[index])
        loads[name].start()

    load("wall", wall.at[0], wallv, 0)
    order = [0, nx - 1] + list(range(1, nx - 1))
    for i, x in enumerate(order):
        load(("coef", x), coef.at[0, :, x], cf.at[:, x], 1 + 2 * i)
        load(("source", x), source.at[0, :, x], psi0.at[:, x], 2 + 2 * i)
    load("flux", flux_in, flux, 1 + 2 * nx)
    load("shape", shape.at[0], tv, 2 + 2 * nx)

    started = []

    def remote(src, dst, send, recv, peer):
        copy = pltpu.make_async_remote_copy(
            src_ref=src, dst_ref=dst, send_sem=send, recv_sem=recv,
            device_id=peer, device_id_type=MESH,
        )
        copy.start()
        return copy

    def spread(stage, slot):
        copies = []
        for d, peer in enumerate(peers[stage]):
            dst = objn.at[nd] if stage == 2 else obj.at[stage, d]
            copies.append(
                remote(own.at[stage], dst, obj_send.at[stage, d], obj_recv.at[stage, d], peer)
            )
        started.extend(copies)
        return copies

    def collect(stage, copies):
        total = own[stage]
        for d, copy in enumerate(copies):
            copy.wait_recv()
            total = total + obj[stage, d]
        return total

    loads["wall"].wait()
    w = wallv[...]
    width = w.shape[1]
    lane_sum = w[:, 0:LANES]
    for k in range(LANES, width, LANES):
        lane_sum = lane_sum + w[:, k:k + LANES]
    own[0] = jnp.sum(lane_sum, axis=0, keepdims=True)

    def start_psi(x, first, count):
        def step(i, carry):
            rows = pl.ds(pl.multiple_of(first + i * 8, 8), 8)
            c1, c2, c3 = cf[1, x, rows, :], cf[2, x, rows, :], cf[3, x, rows, :]
            inverse = 1.0 / (0.5 + cf[0, x, rows, :] + 2.4 * (c1 + c2 + c3))
            cf[1, x, rows, :] = c1 * inverse
            cf[2, x, rows, :] = c2 * inverse
            cf[3, x, rows, :] = c3 * inverse
            for v in range(nv):
                psi0[v, x, rows, :] = psi0[v, x, rows, :] * inverse
            return carry
        lax.fori_loop(0, count // 8, step, 0)

    def plane_copy(field, halo, side, c, send, recv):
        x, peer = (nx - 1, right) if side == 0 else (0, left)
        rows = pl.ds(c * part, part)
        return pltpu.make_async_remote_copy(
            src_ref=field.at[:, x, rows, :], dst_ref=halo.at[side, :, rows, :],
            send_sem=send.at[side, c], recv_sem=recv.at[side, c],
            device_id=peer, device_id_type=MESH,
        )

    sides = ((0, 1, 0, has_left), (1, 0, nx - 1, has_right))

    pl.semaphore_wait(barrier, len(everyone) + beyond)
    for x in (0, nx - 1):
        loads[("coef", x)].wait()
        loads[("source", x)].wait()
    stage_a = spread(0, place)
    for c in range(CHUNKS):
        for came, goes, x, there in sides:
            start_psi(x, c * part, part)
            pl.when(there)(plane_copy(psi0, halo0, goes, c, send0, recv0).start)
    for x in range(1, nx - 1):
        loads[("coef", x)].wait()
        loads[("source", x)].wait()
        start_psi(x, 0, ny)

    def stencil(field, x, v):
        p = field[v, x]
        beside_y, beside_z = shifted_pairs(p)
        if x == 0:
            beside_x = field[v, 1]
        elif x == nx - 1:
            beside_x = field[v, nx - 2]
        else:
            beside_x = field[v, x - 1] + field[v, x + 1]
        return cf[1, x] * beside_x + cf[2, x] * beside_y + cf[3, x] * beside_z

    def first_sweep(x):
        def couple(v, carry):
            mix[v] = stencil(psi0, x, v)
            return carry
        lax.fori_loop(0, nv, couple, 0)

        def combine(i, carry):
            rows = pl.ds(pl.multiple_of(i * ROWS, ROWS), ROWS)
            held = [mix[v, rows, :] for v in range(nv)]
            for o in range(nv):
                total = psi0[o, x, rows, :]
                for v in range(nv):
                    total = total + flux[v, 0, o] * held[v]
                psi1[o, x, rows, :] = total
            return carry
        lax.fori_loop(0, ny // ROWS, combine, 0)

    loads["flux"].wait()
    for x in order:
        first_sweep(x)

    own[1] = collect(0, stage_a)
    stage_b = spread(1, group)

    def join(came, goes, x, c):
        plane_copy(psi0, halo0, came, c, send0, recv0).wait_recv()

        def step(i, carry):
            rows = pl.ds(pl.multiple_of(c * part + i * ROWS, ROWS), ROWS)
            held = [halo0[came, v, rows, :] for v in range(nv)]
            a = cf[1, x, rows, :]
            for o in range(nv):
                total = flux[0, 0, o] * held[0]
                for v in range(1, nv):
                    total = total + flux[v, 0, o] * held[v]
                psi1[o, x, rows, :] = psi1[o, x, rows, :] + a * total
            return carry
        lax.fori_loop(0, part // ROWS, step, 0)
        plane_copy(psi1, halo1, goes, c, send1, recv1).start()

    for c in range(CHUNKS):
        for came, goes, x, there in sides:
            pl.when(there)(functools.partial(join, came, goes, x, c))

    loads["shape"].wait()
    for x in range(nx):
        def adjoint(i, total_sum):
            rows = pl.ds(pl.multiple_of(i * ROWS, ROWS), ROWS)
            held = [tv[v, x, rows, :] for v in range(nv)]
            product = held[0] * psi0[0, x, rows, :]
            for v in range(1, nv):
                product = product + held[v] * psi0[v, x, rows, :]
            for v in range(nv):
                total = flux[v, 0, 0] * held[0]
                for o in range(1, nv):
                    total = total + flux[v, 0, o] * held[o]
                tv[v, x, rows, :] = total
            return total_sum + fold_rows(product)
        acc[x] = lax.fori_loop(0, ny // ROWS, adjoint, jnp.zeros((8, nz), jnp.float32))

    own[2] = collect(1, stage_b)
    objn[nd] = own[2]
    stage_c = spread(2, nd)

    for x in range(nx):
        def last_sweep(v, total):
            return total + fold_rows(tv[v, x] * stencil(psi1, x, v))
        acc[x] = lax.fori_loop(0, nv, last_sweep, acc[x])

    for copy in stage_c:
        copy.wait_recv()
    rows_of = lax.broadcasted_iota(jnp.int32, (nodes, LANES), 0)
    raw = [math.sin(math.pi * (n + 0.5) / nodes) for n in range(nodes)]
    weight = jnp.zeros((nodes, LANES), jnp.float32)
    for n in range(nodes):
        weight = jnp.where(rows_of == n, raw[n] / sum(raw), weight)
    lane_parts = jnp.zeros((nodes, LANES), jnp.float32)
    for n in range(nodes):
        lane_parts = jnp.where(rows_of == n, objn[n], lane_parts)
    objective = jnp.sum(lane_parts, axis=1, keepdims=True) * (1.0 / cells)
    mean_value = jnp.sum(weight * objective, axis=0, keepdims=True)
    variance = jnp.sum(weight * (objective - mean_value) ** 2, axis=0, keepdims=True)
    factor = weight * (1.0 + 2.0 * (objective - mean_value) / jnp.sqrt(variance + 0.25))

    def take(came, x, c):
        plane_copy(psi1, halo1, came, c, send1, recv1).wait_recv()

        def step(i, total):
            rows = pl.ds(pl.multiple_of(c * part + i * ROWS, ROWS), ROWS)
            product = tv[0, x, rows, :] * halo1[came, 0, rows, :]
            for v in range(1, nv):
                product = product + tv[v, x, rows, :] * halo1[came, v, rows, :]
            return total + fold_rows(cf[1, x, rows, :] * product)
        acc[x] = lax.fori_loop(0, part // ROWS, step, acc[x])

    for c in range(CHUNKS):
        for came, goes, x, there in sides:
            pl.when(there)(functools.partial(take, came, x, c))

    for x in range(nx):
        line = jnp.sum(acc[x], axis=0, keepdims=True)
        for k in range(nz // LANES):
            sens[k, x:x + 1, :] = line[:, k * LANES:(k + 1) * LANES]

    width = nz // nodes
    per_tile = LANES // width
    finals = []
    for d, peer in enumerate(peers[2]):
        finals.append(
            remote(
                sens.at[lax.div(peer["node"], per_tile)], fin.at[nd],
                fin_send.at[d], fin_recv.at[d], peer,
            )
        )
    fin[nd] = sens[lax.div(nd, per_tile)]
    for copy in finals:
        copy.wait_recv()
    total = factor[0:1, :] * fin[0]
    for n in range(1, nodes):
        total = total + factor[n:n + 1, :] * fin[n]
    column = lax.rem(nd, per_tile)
    result = total[:, 0:width]
    for k in range(1, per_tile):
        result = jnp.where(column == k, total[:, k * width:(k + 1) * width], result)
    out[...] = result
    for copy in started + finals:
        copy.wait_send()
    for c in range(CHUNKS):
        for came, goes, x, there in sides:
            pl.when(there)(plane_copy(psi0, halo0, goes, c, send0, recv0).wait_send)
            pl.when(there)(plane_copy(psi1, halo1, goes, c, send1, recv1).wait_send)


def solution(mesh):
    nodes, slabs = mesh.shape["node"], mesh.shape["slab"]
    inner = 2 ** (int(math.log2(slabs)) // 2)

    def per_device(source, coef, flux, shape, wall):
        _, nv, nx, ny, nz = source.shape
        f32 = jnp.float32
        dma = pltpu.SemaphoreType.DMA
        hbm = pl.BlockSpec(memory_space=pltpu.HBM)
        most = max(inner, slabs // inner, nodes) - 1
        return pl.pallas_call(
            functools.partial(kernel, nodes, slabs, inner, nx * slabs * nz),
            out_shape=jax.ShapeDtypeStruct((nx, nz // nodes), f32),
            in_specs=[hbm, hbm, hbm, hbm, hbm],
            out_specs=pl.BlockSpec(memory_space=pltpu.VMEM),
            scratch_shapes=[
                pltpu.SMEM((nv, 1, nv), f32),
                pltpu.VMEM((nv, nx, ny, nz), f32),
                pltpu.VMEM((4, nx, ny, nz), f32),
                pltpu.VMEM((nv, nx, ny, nz), f32),
                pltpu.VMEM((nv, ny, nz), f32),
                pltpu.VMEM((nv, nx, ny, nz), f32),
                pltpu.VMEM((2, nv, ny, nz), f32),
                pltpu.VMEM((2, nv, ny, nz), f32),
                pltpu.VMEM((nx, 8, nz), f32),
                pltpu.VMEM((nx, nz), f32),
                pltpu.VMEM((2, most, 1, LANES), f32),
                pltpu.VMEM((nodes, 1, LANES), f32),
                pltpu.VMEM((3, 1, LANES), f32),
                pltpu.VMEM((nz // LANES, nx, LANES), f32),
                pltpu.VMEM((nodes, nx, LANES), f32),
                dma((3 + 2 * nx,)),
                dma((2, CHUNKS)),
                dma((2, CHUNKS)),
                dma((2, CHUNKS)),
                dma((2, CHUNKS)),
                dma((3, most)),
                dma((3, most)),
                dma((nodes - 1,)),
                dma((nodes - 1,)),
            ],
            compiler_params=pltpu.CompilerParams(
                collective_id=0, has_side_effects=True, vmem_limit_bytes=60 * 2 ** 20
            ),
        )(source, coef, jnp.transpose(flux, (1, 0, 2)), shape, wall)

    return jax.shard_map(
        per_device,
        mesh=mesh,
        in_specs=(
            P("node", None, "slab", None, None),
            P("node", None, "slab", None, None),
            P("node", None, None),
            P("node", None, "slab", None, None),
            P("node", "slab", None),
        ),
        out_specs=P("slab", "node"),
        check_vma=False,
    )
```

```python
import functools
import math

import jax
import jax.numpy as jnp
from jax import lax
from jax.experimental import pallas as pl
from jax.experimental.pallas import tpu as pltpu
from jax.sharding import PartitionSpec as P

MESH = pl.DeviceIdType.MESH
CHUNKS = 4
TURNED = 2
DEFERRED = 2
ANSWER = (0, 0)
ROWS = 16
LANES = 128


def shifted_pairs(p):
    ny, nz = p.shape
    row = lax.broadcasted_iota(jnp.int32, p.shape, 0)
    lane = lax.broadcasted_iota(jnp.int32, p.shape, 1)
    above = jnp.where(row == 0, 0.0, pltpu.roll(p, 1, 0))
    below = jnp.where(row == ny - 1, 0.0, pltpu.roll(p, ny - 1, 0))
    before = jnp.where(lane == 0, 0.0, pltpu.roll(p, 1, 1))
    after = jnp.where(lane == nz - 1, 0.0, pltpu.roll(p, nz - 1, 1))
    return above + below, before + after


def fold_rows(block):
    return jnp.sum(jnp.reshape(block, (block.shape[0] // 8, 8, block.shape[1])), axis=0)


def kernel(
    nodes, slabs, inner, cells,
    source, coef, flux_in, shape, wall, out,
    flux, psi0, cf, psi1, mix, tv, halo0, halo1, gsend, gheld, rsend, rheld, plain, aheld, acc, wallv, obj, own, sens, fin,
    load_sem, turn_send, turn_recv, send0, recv0, send1, recv1, obj_send, obj_recv, fin_send, fin_recv,
):
    me, nd = lax.axis_index("slab"), lax.axis_index("node")
    outer = slabs // inner
    place, group = lax.rem(me, inner), lax.div(me, inner)
    has_left, has_right = me > 0, me < slabs - 1
    left, right = {"slab": me - 1}, {"slab": me + 1}
    nv, nx, ny, nz = psi0.shape
    part = ny // CHUNKS

    peers = [
        [{"slab": group * inner + lax.rem(place + d, inner)} for d in range(1, inner)],
        [{"slab": lax.rem(group + d, outer) * inner + place} for d in range(1, outer)],
        [{"node": lax.rem(nd + d, nodes)} for d in range(1, nodes)],
    ]

    barrier = pltpu.get_barrier_semaphore()

    def greet(peer):
        pl.semaphore_signal(barrier, inc=1, device_id=peer, device_id_type=MESH)

    pl.when(has_left & (place == 0))(lambda: greet(left))
    pl.when(has_right & (place == inner - 1))(lambda: greet(right))
    everyone = peers[0] + peers[1] + peers[2]
    for peer in everyone:
        greet(peer)
    beyond = jnp.where(has_left & (place == 0), 1, 0) + jnp.where(has_right & (place == inner - 1), 1, 0)

    loads = {}

    def load(name, src, dst):
        loads[name] = pltpu.make_async_copy(src, dst, load_sem.at[len(loads)])
        loads[name].start()

    load("wall", wall.at[0], wallv)
    cuts = ((0, part), (part, ny - part))
    for k, (first, count) in enumerate(cuts):
        rows = pl.ds(first, count)
        for x in (0, nx - 1):
            load(("coef", x, k), coef.at[0, :, x, rows, :], cf.at[:, x, rows, :])
            load(("source", x, k), source.at[0, :, x, rows, :], psi0.at[:, x, rows, :])

    middle = pl.ds(1, nx - 2)
    load("coef", coef.at[0, :, middle], cf.at[:, middle])
    load("source", source.at[0, :, middle], psi0.at[:, middle])
    load("flux", flux_in, flux)
    load("shape", shape.at[0], tv)
    order = [0, nx - 1] + list(range(1, nx - 1))

    started = []

    def remote(src, dst, send, recv, peer):
        copy = pltpu.make_async_remote_copy(
            src_ref=src, dst_ref=dst, send_sem=send, recv_sem=recv,
            device_id=peer, device_id_type=MESH,
        )
        copy.start()
        return copy

    def spread(stage, slot):
        copies = []
        for d, peer in enumerate(peers[stage]):
            copies.append(
                remote(own.at[stage], obj.at[stage, d], obj_send.at[stage, d], obj_recv.at[stage, d], peer)
            )
        started.extend(copies)
        return copies

    def collect(stage, copies):
        total = own[stage]
        for d, copy in enumerate(copies):
            copy.wait_recv()
            total = total + obj[stage, d]
        return total

    loads["wall"].wait()
    w = wallv[...]
    width = w.shape[1]
    lane_sum = w[:, 0:LANES]
    for k in range(LANES, width, LANES):
        lane_sum = lane_sum + w[:, k:k + LANES]
    own[0] = jnp.sum(lane_sum, axis=0, keepdims=True)

    def start_psi(x, first, count):
        def step(i, carry):
            rows = pl.ds(pl.multiple_of(first + i * 8, 8), 8)
            c1, c2, c3 = cf[1, x, rows, :], cf[2, x, rows, :], cf[3, x, rows, :]
            inverse = 1.0 / (0.5 + cf[0, x, rows, :] + 2.4 * (c1 + c2 + c3))
            cf[1, x, rows, :] = c1 * inverse
            cf[2, x, rows, :] = c2 * inverse
            cf[3, x, rows, :] = c3 * inverse
            for v in range(nv):
                psi0[v, x, rows, :] = psi0[v, x, rows, :] * inverse
            return carry
        lax.fori_loop(0, count // 8, step, 0)

    def plane_copy(field, halo, side, c, send, recv):
        x, peer = (nx - 1, right) if side == 0 else (0, left)
        rows = pl.ds(c * part, part)
        return pltpu.make_async_remote_copy(
            src_ref=field.at[:, x, rows, :], dst_ref=halo.at[side, :, rows, :],
            send_sem=send.at[side, c], recv_sem=recv.at[side, c],
            device_id=peer, device_id_type=MESH,
        )

    sides = ((0, 1, 0, has_left), (1, 0, nx - 1, has_right))

    ends_row, opens_row = has_right & (place == inner - 1), has_left & (place == 0)
    to_left = pltpu.make_async_remote_copy(
        src_ref=gsend, dst_ref=gheld, send_sem=turn_send.at[0], recv_sem=turn_recv.at[0],
        device_id=left, device_id_type=MESH,
    )
    to_right = pltpu.make_async_remote_copy(
        src_ref=rsend, dst_ref=rheld, send_sem=turn_send.at[1], recv_sem=turn_recv.at[1],
        device_id=right, device_id_type=MESH,
    )

    coupling = pltpu.make_async_remote_copy(
        src_ref=cf.at[1, nx - 1], dst_ref=aheld, send_sem=turn_send.at[2],
        recv_sem=turn_recv.at[2], device_id=right, device_id_type=MESH,
    )

    def plain_copy(c):
        rows = pl.ds(c * part, part)
        return pltpu.make_async_remote_copy(
            src_ref=plain.at[:, rows, :], dst_ref=halo1.at[0, :, rows, :],
            send_sem=send1.at[0, c], recv_sem=recv1.at[0, c],
            device_id=right, device_id_type=MESH,
        )

    def send_plain():
        plain[...] = psi1[:, nx - 1]
        for c in range(TURNED, CHUNKS):
            plain_copy(c).start()

    def turn():
        def step(i, carry):
            rows = pl.ds(pl.multiple_of(i * ROWS, ROWS), ROWS)
            a = cf[1, 0, rows, :]
            held = [tv[v, 0, rows, :] for v in range(nv)]
            for v in range(nv):
                total = flux[v, 0, 0] * held[0]
                for o in range(1, nv):
                    total = total + flux[v, 0, o] * held[o]
                gsend[v, rows, :] = a * total
            return carry
        lax.fori_loop(0, TURNED * part // ROWS, step, 0)

    for k in range(len(cuts)):
        for x in (0, nx - 1):
            loads["coef", x, k].wait()
            loads["source", x, k].wait()
    for x in (0, nx - 1):
        start_psi(x, 0, ny)
    loads["flux"].wait()
    loads["shape"].wait()
    pl.when(opens_row)(turn)

    pl.semaphore_wait(barrier, len(everyone) + beyond)
    stage_a = spread(0, place)
    pl.when(opens_row)(to_left.start)
    for c in range(CHUNKS):
        for came, goes, x, there in sides:
            pl.when(there)(plane_copy(psi0, halo0, goes, c, send0, recv0).start)
    pl.when(ends_row)(coupling.start)
    loads["coef"].wait()
    loads["source"].wait()
    for x in range(1, nx - 1):
        start_psi(x, 0, ny)

    def stencil(field, x, v):
        p = field[v, x]
        beside_y, beside_z = shifted_pairs(p)
        if x == 0:
            beside_x = field[v, 1]
        elif x == nx - 1:
            beside_x = field[v, nx - 2]
        else:
            beside_x = field[v, x - 1] + field[v, x + 1]
        return cf[1, x] * beside_x + cf[2, x] * beside_y + cf[3, x] * beside_z

    def first_sweep(x):
        def couple(v, carry):
            mix[v] = stencil(psi0, x, v)
            return carry
        lax.fori_loop(0, nv, couple, 0)

        def combine(i, carry):
            rows = pl.ds(pl.multiple_of(i * ROWS, ROWS), ROWS)
            held = [mix[v, rows, :] for v in range(nv)]
            for o in range(nv):
                total = psi0[o, x, rows, :]
                for v in range(nv):
                    total = total + flux[v, 0, o] * held[v]
                psi1[o, x, rows, :] = total
            return carry
        lax.fori_loop(0, ny // ROWS, combine, 0)

    for x in order:
        first_sweep(x)
    pl.when(ends_row)(send_plain)

    for x in range(nx):
        def adjoint(i, total_sum):
            rows = pl.ds(pl.multiple_of(i * ROWS, ROWS), ROWS)
            held = [tv[v, x, rows, :] for v in range(nv)]
            product = held[0] * psi0[0, x, rows, :]
            for v in range(1, nv):
                product = product + held[v] * psi0[v, x, rows, :]
            for v in range(nv):
                total = flux[v, 0, 0] * held[0]
                for o in range(1, nv):
                    total = total + flux[v, 0, o] * held[o]
                tv[v, x, rows, :] = total
            return total_sum + fold_rows(product)
        acc[x] = lax.fori_loop(0, ny // ROWS, adjoint, jnp.zeros((8, nz), jnp.float32))

    own[1] = collect(0, stage_a)
    stage_b = spread(1, group)

    def join(came, goes, x, c):
        plane_copy(psi0, halo0, came, c, send0, recv0).wait_recv()

        def step(i, carry):
            rows = pl.ds(pl.multiple_of(c * part + i * ROWS, ROWS), ROWS)
            held = [halo0[came, v, rows, :] for v in range(nv)]
            a = cf[1, x, rows, :]
            for o in range(nv):
                total = flux[0, 0, o] * held[0]
                for v in range(1, nv):
                    total = total + flux[v, 0, o] * held[v]
                psi1[o, x, rows, :] = psi1[o, x, rows, :] + a * total
            return carry
        lax.fori_loop(0, part // ROWS, step, 0)
        follow = plane_copy(psi1, halo1, goes, c, send1, recv1)
        if goes == 0:
            pl.when(jnp.logical_not(ends_row))(follow.start)
        elif c >= CHUNKS - DEFERRED:
            pl.when(jnp.logical_not(opens_row))(follow.start)
        else:
            follow.start()

    def answer():
        to_left.wait_recv()

        def step(i, total):
            rows = pl.ds(pl.multiple_of(i * ROWS, ROWS), ROWS)
            product = gheld[0, rows, :] * plain[0, rows, :]
            for v in range(1, nv):
                product = product + gheld[v, rows, :] * plain[v, rows, :]
            return total + fold_rows(product)
        rsend[...] = lax.fori_loop(
            0, TURNED * part // ROWS, step, jnp.zeros((8, nz), jnp.float32)
        )
        to_right.start()

    for c in range(CHUNKS):
        for came, goes, x, there in sides:
            pl.when(there)(functools.partial(join, came, goes, x, c))
            if (came, c) == ANSWER:
                pl.when(ends_row)(answer)

    for x in range(nx):
        def last_sweep(v, total):
            return total + fold_rows(tv[v, x] * stencil(psi1, x, v))
        acc[x] = lax.fori_loop(0, nv, last_sweep, acc[x])

    def take(came, x, c):
        plane_copy(psi1, halo1, came, c, send1, recv1).wait_recv()

        def step(i, total):
            rows = pl.ds(pl.multiple_of(c * part + i * ROWS, ROWS), ROWS)
            product = tv[0, x, rows, :] * halo1[came, 0, rows, :]
            for v in range(1, nv):
                product = product + tv[v, x, rows, :] * halo1[came, v, rows, :]
            return total + fold_rows(cf[1, x, rows, :] * product)
        acc[x] = lax.fori_loop(0, part // ROWS, step, acc[x])

    def add_answer():
        coupling.wait_recv()

        def step(i, total):
            rows = pl.ds(pl.multiple_of(i * ROWS, ROWS), ROWS)
            held = [psi0[v, 0, rows, :] for v in range(nv)]
            product = jnp.zeros((ROWS, nz), jnp.float32)
            for o in range(nv):
                mixed = flux[0, 0, o] * held[0]
                for v in range(1, nv):
                    mixed = mixed + flux[v, 0, o] * held[v]
                product = product + tv[o, 0, rows, :] * mixed
            return total + fold_rows(aheld[rows, :] * cf[1, 0, rows, :] * product)
        added = lax.fori_loop(0, ny // ROWS, step, acc[0])
        to_right.wait_recv()
        acc[0] = added + rheld[...]

    for c in range(CHUNKS):
        for came, goes, x, there in sides:
            if came == 0 and c < TURNED:
                there = there & jnp.logical_not(opens_row)
            pl.when(there)(functools.partial(take, came, x, c))
    pl.when(opens_row)(add_answer)

    for x in range(nx):
        line = jnp.sum(acc[x], axis=0, keepdims=True)
        for k in range(nz // LANES):
            sens[k, x:x + 1, :] = line[:, k * LANES:(k + 1) * LANES]

    objective_part = collect(1, stage_b)
    for k in range(nz // LANES):
        sens[k, nx:8, :] = jnp.broadcast_to(objective_part, (8 - nx, LANES))

    width = nz // nodes
    per_tile = LANES // width
    finals = []
    for d, peer in enumerate(peers[2]):
        finals.append(
            remote(
                sens.at[lax.div(peer["node"], per_tile)], fin.at[nd],
                fin_send.at[d], fin_recv.at[d], peer,
            )
        )
    for c in range(CHUNKS - DEFERRED, CHUNKS):
        pl.when(opens_row)(plane_copy(psi1, halo1, 1, c, send1, recv1).start)
    fin[nd] = sens[lax.div(nd, per_tile)]
    for copy in finals:
        copy.wait_recv()
    rows_of = lax.broadcasted_iota(jnp.int32, (nodes, LANES), 0)
    raw = [math.sin(math.pi * (n + 0.5) / nodes) for n in range(nodes)]
    weight = jnp.zeros((nodes, LANES), jnp.float32)
    for n in range(nodes):
        weight = jnp.where(rows_of == n, raw[n] / sum(raw), weight)
    lane_parts = jnp.zeros((nodes, LANES), jnp.float32)
    for n in range(nodes):
        lane_parts = jnp.where(rows_of == n, fin[n, nx:nx + 1, :], lane_parts)
    objective = jnp.sum(lane_parts, axis=1, keepdims=True) * (1.0 / cells)
    mean_value = jnp.sum(weight * objective, axis=0, keepdims=True)
    variance = jnp.sum(weight * (objective - mean_value) ** 2, axis=0, keepdims=True)
    factor = weight * (1.0 + 2.0 * (objective - mean_value) / jnp.sqrt(variance + 0.25))

    total = factor[0:1, :] * fin[0, 0:nx, :]
    for n in range(1, nodes):
        total = total + factor[n:n + 1, :] * fin[n, 0:nx, :]
    column = lax.rem(nd, per_tile)
    result = total[:, 0:width]
    for k in range(1, per_tile):
        result = jnp.where(column == k, total[:, k * width:(k + 1) * width], result)
    out[...] = result
    for copy in started + finals:
        copy.wait_send()
    for c in range(CHUNKS):
        for came, goes, x, there in sides:
            pl.when(there)(plane_copy(psi0, halo0, goes, c, send0, recv0).wait_send)
            if goes == 0:
                there = there & jnp.logical_not(ends_row)
            pl.when(there)(plane_copy(psi1, halo1, goes, c, send1, recv1).wait_send)
        if c >= TURNED:
            pl.when(ends_row)(plain_copy(c).wait_send)
    pl.when(ends_row)(coupling.wait_send)
    pl.when(opens_row)(to_left.wait_send)
    pl.when(ends_row)(to_right.wait_send)


def solution(mesh):
    nodes, slabs = mesh.shape["node"], mesh.shape["slab"]
    inner = 2 ** (int(math.log2(slabs)) // 2)

    def per_device(source, coef, flux, shape, wall):
        _, nv, nx, ny, nz = source.shape
        f32 = jnp.float32
        dma = pltpu.SemaphoreType.DMA
        hbm = pl.BlockSpec(memory_space=pltpu.HBM)
        most = max(inner, slabs // inner, nodes) - 1
        return pl.pallas_call(
            functools.partial(kernel, nodes, slabs, inner, nx * slabs * nz),
            out_shape=jax.ShapeDtypeStruct((nx, nz // nodes), f32),
            in_specs=[hbm, hbm, hbm, hbm, hbm],
            out_specs=pl.BlockSpec(memory_space=pltpu.VMEM),
            scratch_shapes=[
                pltpu.SMEM((nv, 1, nv), f32),
                pltpu.VMEM((nv, nx, ny, nz), f32),
                pltpu.VMEM((4, nx, ny, nz), f32),
                pltpu.VMEM((nv, nx, ny, nz), f32),
                pltpu.VMEM((nv, ny, nz), f32),
                pltpu.VMEM((nv, nx, ny, nz), f32),
                pltpu.VMEM((2, nv, ny, nz), f32),
                pltpu.VMEM((2, nv, ny, nz), f32),
                pltpu.VMEM((nv, ny * TURNED // CHUNKS, nz), f32),
                pltpu.VMEM((nv, ny * TURNED // CHUNKS, nz), f32),
                pltpu.VMEM((8, nz), f32),
                pltpu.VMEM((8, nz), f32),
                pltpu.VMEM((nv, ny, nz), f32),
                pltpu.VMEM((ny, nz), f32),
                pltpu.VMEM((nx, 8, nz), f32),
                pltpu.VMEM((nx, nz), f32),
                pltpu.VMEM((2, most, 1, LANES), f32),
                pltpu.VMEM((2, 1, LANES), f32),
                pltpu.VMEM((nz // LANES, 8, LANES), f32),
                pltpu.VMEM((nodes, 8, LANES), f32),
                dma((13,)),
                dma((3,)),
                dma((3,)),
                dma((2, CHUNKS)),
                dma((2, CHUNKS)),
                dma((2, CHUNKS)),
                dma((2, CHUNKS)),
                dma((2, most)),
                dma((2, most)),
                dma((nodes - 1,)),
                dma((nodes - 1,)),
            ],
            compiler_params=pltpu.CompilerParams(
                collective_id=0, has_side_effects=True, vmem_limit_bytes=60 * 2 ** 20
            ),
        )(source, coef, jnp.transpose(flux, (1, 0, 2)), shape, wall)

    return jax.shard_map(
        per_device,
        mesh=mesh,
        in_specs=(
            P("node", None, "slab", None, None),
            P("node", None, "slab", None, None),
            P("node", None, None),
            P("node", None, "slab", None, None),
            P("node", "slab", None),
        ),
        out_specs=P("slab", "node"),
        check_vma=False,
    )
```

```python
import functools
import math

import jax
import jax.numpy as jnp
from jax import lax
from jax.experimental import pallas as pl
from jax.experimental.pallas import tpu as pltpu
from jax.sharding import PartitionSpec as P

MESH = pl.DeviceIdType.MESH
CHUNKS = 4
TURNED = 2
DEFERRED = 2
ANSWER = (0, 0)
ROWS = 16
LANES = 128


def shifted_pairs(p):
    ny, nz = p.shape
    row = lax.broadcasted_iota(jnp.int32, p.shape, 0)
    lane = lax.broadcasted_iota(jnp.int32, p.shape, 1)
    above = jnp.where(row == 0, 0.0, pltpu.roll(p, 1, 0))
    below = jnp.where(row == ny - 1, 0.0, pltpu.roll(p, ny - 1, 0))
    before = jnp.where(lane == 0, 0.0, pltpu.roll(p, 1, 1))
    after = jnp.where(lane == nz - 1, 0.0, pltpu.roll(p, nz - 1, 1))
    return above + below, before + after


def fold_rows(block):
    return jnp.sum(jnp.reshape(block, (block.shape[0] // 8, 8, block.shape[1])), axis=0)


def kernel(
    nodes, slabs, inner, cells,
    source, coef, flux_in, shape, wall, out,
    flux, psi0, cf, psi1, mix, tv, halo0, halo1, gsend, gheld, rsend, rheld, plain, aheld, acc, wallv, obj, own, sens, fin,
    load_sem, turn_send, turn_recv, send0, recv0, send1, recv1, obj_send, obj_recv, fin_send, fin_recv,
):
    me, nd = lax.axis_index("slab"), lax.axis_index("node")
    outer = slabs // inner
    place, group = lax.rem(me, inner), lax.div(me, inner)
    has_left, has_right = me > 0, me < slabs - 1
    left, right = {"slab": me - 1}, {"slab": me + 1}
    nv, nx, ny, nz = psi0.shape
    part = ny // CHUNKS

    peers = [
        [{"slab": group * inner + lax.rem(place + d, inner)} for d in range(1, inner)],
        [{"slab": lax.rem(group + d, outer) * inner + place} for d in range(1, outer)],
        [{"node": lax.rem(nd + d, nodes)} for d in range(1, nodes)],
    ]

    barrier = pltpu.get_barrier_semaphore()

    def greet(peer):
        pl.semaphore_signal(barrier, inc=1, device_id=peer, device_id_type=MESH)

    pl.when(has_left & (place == 0))(lambda: greet(left))
    pl.when(has_right & (place == inner - 1))(lambda: greet(right))
    everyone = peers[0] + peers[1] + peers[2]
    for peer in everyone:
        greet(peer)
    beyond = jnp.where(has_left & (place == 0), 1, 0) + jnp.where(has_right & (place == inner - 1), 1, 0)

    loads = {}

    def load(name, src, dst):
        loads[name] = pltpu.make_async_copy(src, dst, load_sem.at[len(loads)])
        loads[name].start()

    load("wall", wall.at[0], wallv)
    cuts = ((0, part), (part, ny - part))
    for k, (first, count) in enumerate(cuts):
        rows = pl.ds(first, count)
        for x in (0, nx - 1):
            load(("coef", x, k), coef.at[0, :, x, rows, :], cf.at[:, x, rows, :])
            load(("source", x, k), source.at[0, :, x, rows, :], psi0.at[:, x, rows, :])

    middle = pl.ds(1, nx - 2)
    load("coef", coef.at[0, :, middle], cf.at[:, middle])
    load("source", source.at[0, :, middle], psi0.at[:, middle])
    load("flux", flux_in, flux)
    load("shape", shape.at[0], tv)
    order = [0, nx - 1] + list(range(1, nx - 1))

    started = []

    def remote(src, dst, send, recv, peer):
        copy = pltpu.make_async_remote_copy(
            src_ref=src, dst_ref=dst, send_sem=send, recv_sem=recv,
            device_id=peer, device_id_type=MESH,
        )
        copy.start()
        return copy

    def spread(stage, slot):
        copies = []
        for d, peer in enumerate(peers[stage]):
            copies.append(
                remote(own.at[stage], obj.at[stage, d], obj_send.at[stage, d], obj_recv.at[stage, d], peer)
            )
        started.extend(copies)
        return copies

    def collect(stage, copies):
        total = own[stage]
        for d, copy in enumerate(copies):
            copy.wait_recv()
            total = total + obj[stage, d]
        return total

    loads["wall"].wait()
    w = wallv[...]
    width = w.shape[1]
    lane_sum = w[:, 0:LANES]
    for k in range(LANES, width, LANES):
        lane_sum = lane_sum + w[:, k:k + LANES]
    own[0] = jnp.sum(lane_sum, axis=0, keepdims=True)

    def start_psi(x, first, count):
        def step(i, carry):
            rows = pl.ds(pl.multiple_of(first + i * 8, 8), 8)
            c1, c2, c3 = cf[1, x, rows, :], cf[2, x, rows, :], cf[3, x, rows, :]
            inverse = 1.0 / (0.5 + cf[0, x, rows, :] + 2.4 * (c1 + c2 + c3))
            cf[1, x, rows, :] = c1 * inverse
            cf[2, x, rows, :] = c2 * inverse
            cf[3, x, rows, :] = c3 * inverse
            for v in range(nv):
                psi0[v, x, rows, :] = psi0[v, x, rows, :] * inverse
            return carry
        lax.fori_loop(0, count // 8, step, 0)

    def plane_copy(field, halo, side, c, send, recv):
        x, peer = (nx - 1, right) if side == 0 else (0, left)
        rows = pl.ds(c * part, part)
        return pltpu.make_async_remote_copy(
            src_ref=field.at[:, x, rows, :], dst_ref=halo.at[side, :, rows, :],
            send_sem=send.at[side, c], recv_sem=recv.at[side, c],
            device_id=peer, device_id_type=MESH,
        )

    sides = ((0, 1, 0, has_left), (1, 0, nx - 1, has_right))

    ends_row, opens_row = has_right & (place == inner - 1), has_left & (place == 0)
    to_left = pltpu.make_async_remote_copy(
        src_ref=gsend, dst_ref=gheld, send_sem=turn_send.at[0], recv_sem=turn_recv.at[0],
        device_id=left, device_id_type=MESH,
    )
    to_right = pltpu.make_async_remote_copy(
        src_ref=rsend, dst_ref=rheld, send_sem=turn_send.at[1], recv_sem=turn_recv.at[1],
        device_id=right, device_id_type=MESH,
    )

    coupling = pltpu.make_async_remote_copy(
        src_ref=cf.at[1, nx - 1], dst_ref=aheld, send_sem=turn_send.at[2],
        recv_sem=turn_recv.at[2], device_id=right, device_id_type=MESH,
    )

    def plain_copy(c):
        rows = pl.ds(c * part, part)
        return pltpu.make_async_remote_copy(
            src_ref=plain.at[:, rows, :], dst_ref=halo1.at[0, :, rows, :],
            send_sem=send1.at[0, c], recv_sem=recv1.at[0, c],
            device_id=right, device_id_type=MESH,
        )

    def send_plain():
        plain[...] = psi1[:, nx - 1]
        for c in range(TURNED, CHUNKS):
            plain_copy(c).start()

    def turn():
        def step(i, carry):
            rows = pl.ds(pl.multiple_of(i * ROWS, ROWS), ROWS)
            a = cf[1, 0, rows, :]
            held = [tv[v, 0, rows, :] for v in range(nv)]
            for v in range(nv):
                total = flux[v, 0, 0] * held[0]
                for o in range(1, nv):
                    total = total + flux[v, 0, o] * held[o]
                gsend[v, rows, :] = a * total
            return carry
        lax.fori_loop(0, TURNED * part // ROWS, step, 0)

    for k in range(len(cuts)):
        for x in (0, nx - 1):
            loads["coef", x, k].wait()
            loads["source", x, k].wait()
    for x in (0, nx - 1):
        start_psi(x, 0, ny)
    loads["flux"].wait()
    loads["shape"].wait()
    pl.when(opens_row)(turn)

    pl.semaphore_wait(barrier, len(everyone) + beyond)
    pl.when(opens_row)(to_left.start)
    for c in range(CHUNKS):
        for came, goes, x, there in sides:
            pl.when(there)(plane_copy(psi0, halo0, goes, c, send0, recv0).start)
        if c == 0:
            stage_a = spread(0, place)
    pl.when(ends_row)(coupling.start)
    loads["coef"].wait()
    loads["source"].wait()
    for x in range(1, nx - 1):
        start_psi(x, 0, ny)

    def stencil(field, x, v):
        p = field[v, x]
        beside_y, beside_z = shifted_pairs(p)
        if x == 0:
            beside_x = field[v, 1]
        elif x == nx - 1:
            beside_x = field[v, nx - 2]
        else:
            beside_x = field[v, x - 1] + field[v, x + 1]
        return cf[1, x] * beside_x + cf[2, x] * beside_y + cf[3, x] * beside_z

    def first_sweep(x):
        def couple(v, carry):
            mix[v] = stencil(psi0, x, v)
            return carry
        lax.fori_loop(0, nv, couple, 0)

        def combine(i, carry):
            rows = pl.ds(pl.multiple_of(i * ROWS, ROWS), ROWS)
            held = [mix[v, rows, :] for v in range(nv)]
            for o in range(nv):
                total = psi0[o, x, rows, :]
                for v in range(nv):
                    total = total + flux[v, 0, o] * held[v]
                psi1[o, x, rows, :] = total
            return carry
        lax.fori_loop(0, ny // ROWS, combine, 0)

    for x in order:
        first_sweep(x)
    pl.when(ends_row)(send_plain)

    for x in range(nx):
        def adjoint(i, total_sum):
            rows = pl.ds(pl.multiple_of(i * ROWS, ROWS), ROWS)
            held = [tv[v, x, rows, :] for v in range(nv)]
            product = held[0] * psi0[0, x, rows, :]
            for v in range(1, nv):
                product = product + held[v] * psi0[v, x, rows, :]
            for v in range(nv):
                total = flux[v, 0, 0] * held[0]
                for o in range(1, nv):
                    total = total + flux[v, 0, o] * held[o]
                tv[v, x, rows, :] = total
            return total_sum + fold_rows(product)
        acc[x] = lax.fori_loop(0, ny // ROWS, adjoint, jnp.zeros((8, nz), jnp.float32))

    own[1] = collect(0, stage_a)
    stage_b = spread(1, group)

    def join(came, goes, x, c):
        plane_copy(psi0, halo0, came, c, send0, recv0).wait_recv()

        def step(i, carry):
            rows = pl.ds(pl.multiple_of(c * part + i * ROWS, ROWS), ROWS)
            held = [halo0[came, v, rows, :] for v in range(nv)]
            a = cf[1, x, rows, :]
            for o in range(nv):
                total = flux[0, 0, o] * held[0]
                for v in range(1, nv):
                    total = total + flux[v, 0, o] * held[v]
                psi1[o, x, rows, :] = psi1[o, x, rows, :] + a * total
            return carry
        lax.fori_loop(0, part // ROWS, step, 0)
        follow = plane_copy(psi1, halo1, goes, c, send1, recv1)
        if goes == 0:
            pl.when(jnp.logical_not(ends_row))(follow.start)
        elif c >= CHUNKS - DEFERRED:
            pl.when(jnp.logical_not(opens_row))(follow.start)
        else:
            follow.start()

    def answer():
        to_left.wait_recv()

        def step(i, total):
            rows = pl.ds(pl.multiple_of(i * ROWS, ROWS), ROWS)
            product = gheld[0, rows, :] * plain[0, rows, :]
            for v in range(1, nv):
                product = product + gheld[v, rows, :] * plain[v, rows, :]
            return total + fold_rows(product)
        rsend[...] = lax.fori_loop(
            0, TURNED * part // ROWS, step, jnp.zeros((8, nz), jnp.float32)
        )
        to_right.start()

    for c in range(CHUNKS):
        for came, goes, x, there in sides:
            pl.when(there)(functools.partial(join, came, goes, x, c))
            if (came, c) == ANSWER:
                pl.when(ends_row)(answer)

    for x in range(nx):
        def last_sweep(v, total):
            return total + fold_rows(tv[v, x] * stencil(psi1, x, v))
        acc[x] = lax.fori_loop(0, nv, last_sweep, acc[x])

    def take(came, x, c):
        plane_copy(psi1, halo1, came, c, send1, recv1).wait_recv()

        def step(i, total):
            rows = pl.ds(pl.multiple_of(c * part + i * ROWS, ROWS), ROWS)
            product = tv[0, x, rows, :] * halo1[came, 0, rows, :]
            for v in range(1, nv):
                product = product + tv[v, x, rows, :] * halo1[came, v, rows, :]
            return total + fold_rows(cf[1, x, rows, :] * product)
        acc[x] = lax.fori_loop(0, part // ROWS, step, acc[x])

    def add_answer():
        coupling.wait_recv()

        def step(i, total):
            rows = pl.ds(pl.multiple_of(i * ROWS, ROWS), ROWS)
            held = [psi0[v, 0, rows, :] for v in range(nv)]
            product = jnp.zeros((ROWS, nz), jnp.float32)
            for o in range(nv):
                mixed = flux[0, 0, o] * held[0]
                for v in range(1, nv):
                    mixed = mixed + flux[v, 0, o] * held[v]
                product = product + tv[o, 0, rows, :] * mixed
            return total + fold_rows(aheld[rows, :] * cf[1, 0, rows, :] * product)
        added = lax.fori_loop(0, ny // ROWS, step, acc[0])
        to_right.wait_recv()
        acc[0] = added + rheld[...]

    for c in range(CHUNKS):
        for came, goes, x, there in sides:
            if came == 0 and c < TURNED:
                there = there & jnp.logical_not(opens_row)
            pl.when(there)(functools.partial(take, came, x, c))
    pl.when(opens_row)(add_answer)

    for x in range(nx):
        line = jnp.sum(acc[x], axis=0, keepdims=True)
        for k in range(nz // LANES):
            sens[k, x:x + 1, :] = line[:, k * LANES:(k + 1) * LANES]

    objective_part = collect(1, stage_b)
    for k in range(nz // LANES):
        sens[k, nx:8, :] = jnp.broadcast_to(objective_part, (8 - nx, LANES))

    width = nz // nodes
    per_tile = LANES // width
    finals = []
    for d, peer in enumerate(peers[2]):
        finals.append(
            remote(
                sens.at[lax.div(peer["node"], per_tile)], fin.at[nd],
                fin_send.at[d], fin_recv.at[d], peer,
            )
        )
    for c in range(CHUNKS - DEFERRED, CHUNKS):
        pl.when(opens_row)(plane_copy(psi1, halo1, 1, c, send1, recv1).start)
    fin[nd] = sens[lax.div(nd, per_tile)]
    for copy in finals:
        copy.wait_recv()
    rows_of = lax.broadcasted_iota(jnp.int32, (nodes, LANES), 0)
    raw = [math.sin(math.pi * (n + 0.5) / nodes) for n in range(nodes)]
    weight = jnp.zeros((nodes, LANES), jnp.float32)
    for n in range(nodes):
        weight = jnp.where(rows_of == n, raw[n] / sum(raw), weight)
    lane_parts = jnp.zeros((nodes, LANES), jnp.float32)
    for n in range(nodes):
        lane_parts = jnp.where(rows_of == n, fin[n, nx:nx + 1, :], lane_parts)
    objective = jnp.sum(lane_parts, axis=1, keepdims=True) * (1.0 / cells)
    mean_value = jnp.sum(weight * objective, axis=0, keepdims=True)
    variance = jnp.sum(weight * (objective - mean_value) ** 2, axis=0, keepdims=True)
    factor = weight * (1.0 + 2.0 * (objective - mean_value) / jnp.sqrt(variance + 0.25))

    total = factor[0:1, :] * fin[0, 0:nx, :]
    for n in range(1, nodes):
        total = total + factor[n:n + 1, :] * fin[n, 0:nx, :]
    column = lax.rem(nd, per_tile)
    result = total[:, 0:width]
    for k in range(1, per_tile):
        result = jnp.where(column == k, total[:, k * width:(k + 1) * width], result)
    out[...] = result
    for copy in started + finals:
        copy.wait_send()
    for c in range(CHUNKS):
        for came, goes, x, there in sides:
            pl.when(there)(plane_copy(psi0, halo0, goes, c, send0, recv0).wait_send)
            if goes == 0:
                there = there & jnp.logical_not(ends_row)
            pl.when(there)(plane_copy(psi1, halo1, goes, c, send1, recv1).wait_send)
        if c >= TURNED:
            pl.when(ends_row)(plain_copy(c).wait_send)
    pl.when(ends_row)(coupling.wait_send)
    pl.when(opens_row)(to_left.wait_send)
    pl.when(ends_row)(to_right.wait_send)


def solution(mesh):
    nodes, slabs = mesh.shape["node"], mesh.shape["slab"]
    inner = 2 ** (int(math.log2(slabs)) // 2)

    def per_device(source, coef, flux, shape, wall):
        _, nv, nx, ny, nz = source.shape
        f32 = jnp.float32
        dma = pltpu.SemaphoreType.DMA
        hbm = pl.BlockSpec(memory_space=pltpu.HBM)
        most = max(inner, slabs // inner, nodes) - 1
        return pl.pallas_call(
            functools.partial(kernel, nodes, slabs, inner, nx * slabs * nz),
            out_shape=jax.ShapeDtypeStruct((nx, nz // nodes), f32),
            in_specs=[hbm, hbm, hbm, hbm, hbm],
            out_specs=pl.BlockSpec(memory_space=pltpu.VMEM),
            scratch_shapes=[
                pltpu.SMEM((nv, 1, nv), f32),
                pltpu.VMEM((nv, nx, ny, nz), f32),
                pltpu.VMEM((4, nx, ny, nz), f32),
                pltpu.VMEM((nv, nx, ny, nz), f32),
                pltpu.VMEM((nv, ny, nz), f32),
                pltpu.VMEM((nv, nx, ny, nz), f32),
                pltpu.VMEM((2, nv, ny, nz), f32),
                pltpu.VMEM((2, nv, ny, nz), f32),
                pltpu.VMEM((nv, ny * TURNED // CHUNKS, nz), f32),
                pltpu.VMEM((nv, ny * TURNED // CHUNKS, nz), f32),
                pltpu.VMEM((8, nz), f32),
                pltpu.VMEM((8, nz), f32),
                pltpu.VMEM((nv, ny, nz), f32),
                pltpu.VMEM((ny, nz), f32),
                pltpu.VMEM((nx, 8, nz), f32),
                pltpu.VMEM((nx, nz), f32),
                pltpu.VMEM((2, most, 1, LANES), f32),
                pltpu.VMEM((2, 1, LANES), f32),
                pltpu.VMEM((nz // LANES, 8, LANES), f32),
                pltpu.VMEM((nodes, 8, LANES), f32),
                dma((13,)),
                dma((3,)),
                dma((3,)),
                dma((2, CHUNKS)),
                dma((2, CHUNKS)),
                dma((2, CHUNKS)),
                dma((2, CHUNKS)),
                dma((2, most)),
                dma((2, most)),
                dma((nodes - 1,)),
                dma((nodes - 1,)),
            ],
            compiler_params=pltpu.CompilerParams(
                collective_id=0, has_side_effects=True, vmem_limit_bytes=56551424
            ),
        )(source, coef, jnp.transpose(flux, (1, 0, 2)), shape, wall)

    return jax.shard_map(
        per_device,
        mesh=mesh,
        in_specs=(
            P("node", None, "slab", None, None),
            P("node", None, "slab", None, None),
            P("node", None, None),
            P("node", None, "slab", None, None),
            P("node", "slab", None),
        ),
        out_specs=P("slab", "node"),
        check_vma=False,
    )
```

```python
import functools
import math

import jax
import jax.numpy as jnp
from jax import lax
from jax.experimental import pallas as pl
from jax.experimental.pallas import tpu as pltpu
from jax.sharding import PartitionSpec as P

MESH = pl.DeviceIdType.MESH
CHUNKS = 4
TURNED = 2
DEFERRED = 2
ANSWER = (0, 0)
ROWS = 16
LANES = 128


def shifted_pairs(p):
    ny, nz = p.shape
    row = lax.broadcasted_iota(jnp.int32, p.shape, 0)
    lane = lax.broadcasted_iota(jnp.int32, p.shape, 1)
    above = jnp.where(row == 0, 0.0, pltpu.roll(p, 1, 0))
    below = jnp.where(row == ny - 1, 0.0, pltpu.roll(p, ny - 1, 0))
    before = jnp.where(lane == 0, 0.0, pltpu.roll(p, 1, 1))
    after = jnp.where(lane == nz - 1, 0.0, pltpu.roll(p, nz - 1, 1))
    return above + below, before + after


def fold_rows(block):
    return jnp.sum(jnp.reshape(block, (block.shape[0] // 8, 8, block.shape[1])), axis=0)


def kernel(
    nodes, slabs, inner, cells,
    source, coef, flux_in, shape, wall, out,
    flux, psi0, cf, psi1, mix, tv, halo0, halo1, gsend, gheld, rsend, rheld, plain, aheld, acc, wallv, obj, own, sens, fin,
    entered, load_sem, turn_send, turn_recv, send0, recv0, send1, recv1, obj_send, obj_recv, fin_send, fin_recv,
):
    me, nd = lax.axis_index("slab"), lax.axis_index("node")
    outer = slabs // inner
    place, group = lax.rem(me, inner), lax.div(me, inner)
    has_left, has_right = me > 0, me < slabs - 1
    left, right = {"slab": me - 1}, {"slab": me + 1}
    nv, nx, ny, nz = psi0.shape
    part = ny // CHUNKS

    peers = [
        [{"slab": group * inner + lax.rem(place + d, inner)} for d in range(1, inner)],
        [{"slab": lax.rem(group + d, outer) * inner + place} for d in range(1, outer)],
        [{"node": lax.rem(nd + d, nodes)} for d in range(1, nodes)],
    ]

    barrier = pltpu.get_barrier_semaphore()

    def greet(peer):
        pl.semaphore_signal(barrier, inc=1, device_id=peer, device_id_type=MESH)

    pl.when(has_left & (place == 0))(lambda: greet(left))
    pl.when(has_right & (place == inner - 1))(lambda: greet(right))
    near = list(peers[2]) if nodes < 8 else [
        {"node": nd + 1 - 2 * lax.rem(nd, 2)},
        {"node": lax.rem(nd + 2, nodes)},
        {"node": lax.rem(nd + nodes - 2, nodes)},
    ]
    if outer < 8:
        near += peers[1]
    else:
        half = outer // 2
        row, line = lax.div(group, half), lax.rem(group, half)
        for spot in (
            row * half + lax.rem(line + 1, half),
            row * half + lax.rem(line + half - 1, half),
            (1 - row) * half + line,
        ):
            near.append({"slab": spot * inner + place})
    everyone = peers[0] + near
    for peer in everyone:
        greet(peer)
    beyond = jnp.where(has_left & (place == 0), 1, 0) + jnp.where(has_right & (place == inner - 1), 1, 0)

    loads = {}

    def load(name, src, dst):
        loads[name] = pltpu.make_async_copy(src, dst, load_sem.at[len(loads)])
        loads[name].start()

    load("wall", wall.at[0], wallv)
    cuts = ((0, part), (part, ny - part))
    for k, (first, count) in enumerate(cuts):
        rows = pl.ds(first, count)
        for x in (0, nx - 1):
            load(("coef", x, k), coef.at[0, :, x, rows, :], cf.at[:, x, rows, :])
            load(("source", x, k), source.at[0, :, x, rows, :], psi0.at[:, x, rows, :])

    middle = pl.ds(1, nx - 2)
    load("coef", coef.at[0, :, middle], cf.at[:, middle])
    load("source", source.at[0, :, middle], psi0.at[:, middle])
    load("flux", flux_in, flux)
    load("shape", shape.at[0], tv)
    order = [0, nx - 1] + list(range(1, nx - 1))

    def tell(k):
        for peer in near:
            pl.semaphore_signal(entered.at[k], inc=1, device_id=peer, device_id_type=MESH)

    def hear(k):
        pl.semaphore_wait(entered.at[k], len(near))

    started = []

    def remote(src, dst, send, recv, peer):
        copy = pltpu.make_async_remote_copy(
            src_ref=src, dst_ref=dst, send_sem=send, recv_sem=recv,
            device_id=peer, device_id_type=MESH,
        )
        copy.start()
        return copy

    def spread(stage, slot):
        copies = []
        for d, peer in enumerate(peers[stage]):
            copies.append(
                remote(own.at[stage], obj.at[stage, d], obj_send.at[stage, d], obj_recv.at[stage, d], peer)
            )
        started.extend(copies)
        return copies

    def collect(stage, copies):
        total = own[stage]
        for d, copy in enumerate(copies):
            copy.wait_recv()
            total = total + obj[stage, d]
        return total

    loads["wall"].wait()
    w = wallv[...]
    width = w.shape[1]
    lane_sum = w[:, 0:LANES]
    for k in range(LANES, width, LANES):
        lane_sum = lane_sum + w[:, k:k + LANES]
    own[0] = jnp.sum(lane_sum, axis=0, keepdims=True)

    def start_psi(x, first, count):
        def step(i, carry):
            rows = pl.ds(pl.multiple_of(first + i * 8, 8), 8)
            c1, c2, c3 = cf[1, x, rows, :], cf[2, x, rows, :], cf[3, x, rows, :]
            inverse = 1.0 / (0.5 + cf[0, x, rows, :] + 2.4 * (c1 + c2 + c3))
            cf[1, x, rows, :] = c1 * inverse
            cf[2, x, rows, :] = c2 * inverse
            cf[3, x, rows, :] = c3 * inverse
            for v in range(nv):
                psi0[v, x, rows, :] = psi0[v, x, rows, :] * inverse
            return carry
        lax.fori_loop(0, count // 8, step, 0)

    def plane_copy(field, halo, side, c, send, recv):
        x, peer = (nx - 1, right) if side == 0 else (0, left)
        rows = pl.ds(c * part, part)
        return pltpu.make_async_remote_copy(
            src_ref=field.at[:, x, rows, :], dst_ref=halo.at[side, :, rows, :],
            send_sem=send.at[side, c], recv_sem=recv.at[side, c],
            device_id=peer, device_id_type=MESH,
        )

    sides = ((0, 1, 0, has_left), (1, 0, nx - 1, has_right))

    ends_row, opens_row = has_right & (place == inner - 1), has_left & (place == 0)
    to_left = pltpu.make_async_remote_copy(
        src_ref=gsend, dst_ref=gheld, send_sem=turn_send.at[0], recv_sem=turn_recv.at[0],
        device_id=left, device_id_type=MESH,
    )
    to_right = pltpu.make_async_remote_copy(
        src_ref=rsend, dst_ref=rheld, send_sem=turn_send.at[1], recv_sem=turn_recv.at[1],
        device_id=right, device_id_type=MESH,
    )

    coupling = pltpu.make_async_remote_copy(
        src_ref=cf.at[1, nx - 1], dst_ref=aheld, send_sem=turn_send.at[2],
        recv_sem=turn_recv.at[2], device_id=right, device_id_type=MESH,
    )

    def plain_copy(c):
        rows = pl.ds(c * part, part)
        return pltpu.make_async_remote_copy(
            src_ref=plain.at[:, rows, :], dst_ref=halo1.at[0, :, rows, :],
            send_sem=send1.at[0, c], recv_sem=recv1.at[0, c],
            device_id=right, device_id_type=MESH,
        )

    def send_plain():
        plain[...] = psi1[:, nx - 1]
        for c in range(TURNED, CHUNKS):
            plain_copy(c).start()

    def turn():
        loads["flux"].wait()
        loads["shape"].wait()

        def step(i, carry):
            rows = pl.ds(pl.multiple_of(i * ROWS, ROWS), ROWS)
            a = cf[1, 0, rows, :]
            held = [tv[v, 0, rows, :] for v in range(nv)]
            for v in range(nv):
                total = flux[v, 0, 0] * held[0]
                for o in range(1, nv):
                    total = total + flux[v, 0, o] * held[o]
                gsend[v, rows, :] = a * total
            return carry
        lax.fori_loop(0, TURNED * part // ROWS, step, 0)

    for k in range(len(cuts)):
        for x in (0, nx - 1):
            loads["coef", x, k].wait()
            loads["source", x, k].wait()
    for x in (0, nx - 1):
        start_psi(x, 0, ny)
    pl.when(opens_row)(turn)

    pl.semaphore_wait(barrier, len(everyone) + beyond)
    pl.when(opens_row)(to_left.start)
    for c in range(CHUNKS):
        for came, goes, x, there in sides:
            pl.when(there)(plane_copy(psi0, halo0, goes, c, send0, recv0).start)
        if c == 0:
            stage_a = spread(0, place)
    pl.when(ends_row)(coupling.start)
    tell(0)
    loads["coef"].wait()
    loads["source"].wait()
    for x in range(1, nx - 1):
        start_psi(x, 0, ny)

    def stencil(field, x, v):
        p = field[v, x]
        beside_y, beside_z = shifted_pairs(p)
        if x == 0:
            beside_x = field[v, 1]
        elif x == nx - 1:
            beside_x = field[v, nx - 2]
        else:
            beside_x = field[v, x - 1] + field[v, x + 1]
        return cf[1, x] * beside_x + cf[2, x] * beside_y + cf[3, x] * beside_z

    def first_sweep(x):
        def couple(v, carry):
            mix[v] = stencil(psi0, x, v)
            return carry
        lax.fori_loop(0, nv, couple, 0)

        def combine(i, carry):
            rows = pl.ds(pl.multiple_of(i * ROWS, ROWS), ROWS)
            held = [mix[v, rows, :] for v in range(nv)]
            for o in range(nv):
                total = psi0[o, x, rows, :]
                for v in range(nv):
                    total = total + flux[v, 0, o] * held[v]
                psi1[o, x, rows, :] = total
            return carry
        lax.fori_loop(0, ny // ROWS, combine, 0)

    others = jnp.logical_not(opens_row)
    pl.when(others)(loads["flux"].wait)
    for x in order:
        first_sweep(x)
    pl.when(ends_row)(send_plain)
    hear(0)
    tell(1)

    pl.when(others)(loads["shape"].wait)

    for x in range(nx):
        def adjoint(i, total_sum):
            rows = pl.ds(pl.multiple_of(i * ROWS, ROWS), ROWS)
            held = [tv[v, x, rows, :] for v in range(nv)]
            product = held[0] * psi0[0, x, rows, :]
            for v in range(1, nv):
                product = product + held[v] * psi0[v, x, rows, :]
            for v in range(nv):
                total = flux[v, 0, 0] * held[0]
                for o in range(1, nv):
                    total = total + flux[v, 0, o] * held[o]
                tv[v, x, rows, :] = total
            return total_sum + fold_rows(product)
        acc[x] = lax.fori_loop(0, ny // ROWS, adjoint, jnp.zeros((8, nz), jnp.float32))

    own[1] = collect(0, stage_a)
    hear(1)
    stage_b = spread(1, group)

    def join(came, goes, x, c):
        plane_copy(psi0, halo0, came, c, send0, recv0).wait_recv()

        def step(i, carry):
            rows = pl.ds(pl.multiple_of(c * part + i * ROWS, ROWS), ROWS)
            held = [halo0[came, v, rows, :] for v in range(nv)]
            a = cf[1, x, rows, :]
            for o in range(nv):
                total = flux[0, 0, o] * held[0]
                for v in range(1, nv):
                    total = total + flux[v, 0, o] * held[v]
                psi1[o, x, rows, :] = psi1[o, x, rows, :] + a * total
            return carry
        lax.fori_loop(0, part // ROWS, step, 0)
        follow = plane_copy(psi1, halo1, goes, c, send1, recv1)
        if goes == 0:
            pl.when(jnp.logical_not(ends_row))(follow.start)
        elif c >= CHUNKS - DEFERRED:
            pl.when(jnp.logical_not(opens_row))(follow.start)
        else:
            follow.start()

    def answer():
        to_left.wait_recv()

        def step(i, total):
            rows = pl.ds(pl.multiple_of(i * ROWS, ROWS), ROWS)
            product = gheld[0, rows, :] * plain[0, rows, :]
            for v in range(1, nv):
                product = product + gheld[v, rows, :] * plain[v, rows, :]
            return total + fold_rows(product)
        rsend[...] = lax.fori_loop(
            0, TURNED * part // ROWS, step, jnp.zeros((8, nz), jnp.float32)
        )
        to_right.start()

    for c in range(CHUNKS):
        for came, goes, x, there in sides:
            pl.when(there)(functools.partial(join, came, goes, x, c))
            if (came, c) == ANSWER:
                pl.when(ends_row)(answer)

    for x in range(nx):
        def last_sweep(v, total):
            return total + fold_rows(tv[v, x] * stencil(psi1, x, v))
        acc[x] = lax.fori_loop(0, nv, last_sweep, acc[x])

    def take(came, x, c):
        plane_copy(psi1, halo1, came, c, send1, recv1).wait_recv()

        def step(i, total):
            rows = pl.ds(pl.multiple_of(c * part + i * ROWS, ROWS), ROWS)
            product = tv[0, x, rows, :] * halo1[came, 0, rows, :]
            for v in range(1, nv):
                product = product + tv[v, x, rows, :] * halo1[came, v, rows, :]
            return total + fold_rows(cf[1, x, rows, :] * product)
        acc[x] = lax.fori_loop(0, part // ROWS, step, acc[x])

    def add_own():
        coupling.wait_recv()

        def step(i, total):
            rows = pl.ds(pl.multiple_of(i * ROWS, ROWS), ROWS)
            held = [psi0[v, 0, rows, :] for v in range(nv)]
            product = jnp.zeros((ROWS, nz), jnp.float32)
            for o in range(nv):
                mixed = flux[0, 0, o] * held[0]
                for v in range(1, nv):
                    mixed = mixed + flux[v, 0, o] * held[v]
                product = product + tv[o, 0, rows, :] * mixed
            return total + fold_rows(aheld[rows, :] * cf[1, 0, rows, :] * product)
        acc[0] = lax.fori_loop(0, ny // ROWS, step, acc[0])

    def add_answer():
        to_right.wait_recv()
        acc[0] = acc[0] + rheld[...]

    pl.when(opens_row)(add_own)

    for c in range(CHUNKS):
        for came, goes, x, there in sides:
            if came == 0 and c < TURNED:
                there = there & jnp.logical_not(opens_row)
            pl.when(there)(functools.partial(take, came, x, c))
    pl.when(opens_row)(add_answer)

    for x in range(nx):
        line = jnp.sum(acc[x], axis=0, keepdims=True)
        for k in range(nz // LANES):
            sens[k, x:x + 1, :] = line[:, k * LANES:(k + 1) * LANES]

    objective_part = collect(1, stage_b)
    for k in range(nz // LANES):
        sens[k, nx:8, :] = jnp.broadcast_to(objective_part, (8 - nx, LANES))

    width = nz // nodes
    per_tile = LANES // width
    finals = []
    for d, peer in enumerate(peers[2]):
        finals.append(
            remote(
                sens.at[lax.div(peer["node"], per_tile)], fin.at[nd],
                fin_send.at[d], fin_recv.at[d], peer,
            )
        )
    for c in range(CHUNKS - DEFERRED, CHUNKS):
        pl.when(opens_row)(plane_copy(psi1, halo1, 1, c, send1, recv1).start)
    fin[nd] = sens[lax.div(nd, per_tile)]
    for copy in finals:
        copy.wait_recv()
    rows_of = lax.broadcasted_iota(jnp.int32, (nodes, LANES), 0)
    raw = [math.sin(math.pi * (n + 0.5) / nodes) for n in range(nodes)]
    weight = jnp.zeros((nodes, LANES), jnp.float32)
    for n in range(nodes):
        weight = jnp.where(rows_of == n, raw[n] / sum(raw), weight)
    lane_parts = jnp.zeros((nodes, LANES), jnp.float32)
    for n in range(nodes):
        lane_parts = jnp.where(rows_of == n, fin[n, nx:nx + 1, :], lane_parts)
    objective = jnp.sum(lane_parts, axis=1, keepdims=True) * (1.0 / cells)
    mean_value = jnp.sum(weight * objective, axis=0, keepdims=True)
    variance = jnp.sum(weight * (objective - mean_value) ** 2, axis=0, keepdims=True)
    factor = weight * (1.0 + 2.0 * (objective - mean_value) / jnp.sqrt(variance + 0.25))

    total = factor[0:1, :] * fin[0, 0:nx, :]
    for n in range(1, nodes):
        total = total + factor[n:n + 1, :] * fin[n, 0:nx, :]
    column = lax.rem(nd, per_tile)
    result = total[:, 0:width]
    for k in range(1, per_tile):
        result = jnp.where(column == k, total[:, k * width:(k + 1) * width], result)
    out[...] = result
    for copy in started + finals:
        copy.wait_send()
    for c in range(CHUNKS):
        for came, goes, x, there in sides:
            pl.when(there)(plane_copy(psi0, halo0, goes, c, send0, recv0).wait_send)
            if goes == 0:
                there = there & jnp.logical_not(ends_row)
            pl.when(there)(plane_copy(psi1, halo1, goes, c, send1, recv1).wait_send)
        if c >= TURNED:
            pl.when(ends_row)(plain_copy(c).wait_send)
    pl.when(ends_row)(coupling.wait_send)
    pl.when(opens_row)(to_left.wait_send)
    pl.when(ends_row)(to_right.wait_send)


def solution(mesh):
    nodes, slabs = mesh.shape["node"], mesh.shape["slab"]
    inner = 2 ** (int(math.log2(slabs)) // 2)

    def per_device(source, coef, flux, shape, wall):
        _, nv, nx, ny, nz = source.shape
        f32 = jnp.float32
        dma = pltpu.SemaphoreType.DMA
        hbm = pl.BlockSpec(memory_space=pltpu.HBM)
        most = max(inner, slabs // inner, nodes) - 1
        return pl.pallas_call(
            functools.partial(kernel, nodes, slabs, inner, nx * slabs * nz),
            out_shape=jax.ShapeDtypeStruct((nx, nz // nodes), f32),
            in_specs=[hbm, hbm, hbm, hbm, hbm],
            out_specs=pl.BlockSpec(memory_space=pltpu.VMEM),
            scratch_shapes=[
                pltpu.SMEM((nv, 1, nv), f32),
                pltpu.VMEM((nv, nx, ny, nz), f32),
                pltpu.VMEM((4, nx, ny, nz), f32),
                pltpu.VMEM((nv, nx, ny, nz), f32),
                pltpu.VMEM((nv, ny, nz), f32),
                pltpu.VMEM((nv, nx, ny, nz), f32),
                pltpu.VMEM((2, nv, ny, nz), f32),
                pltpu.VMEM((2, nv, ny, nz), f32),
                pltpu.VMEM((nv, ny * TURNED // CHUNKS, nz), f32),
                pltpu.VMEM((nv, ny * TURNED // CHUNKS, nz), f32),
                pltpu.VMEM((8, nz), f32),
                pltpu.VMEM((8, nz), f32),
                pltpu.VMEM((nv, ny, nz), f32),
                pltpu.VMEM((ny, nz), f32),
                pltpu.VMEM((nx, 8, nz), f32),
                pltpu.VMEM((nx, nz), f32),
                pltpu.VMEM((2, most, 1, LANES), f32),
                pltpu.VMEM((2, 1, LANES), f32),
                pltpu.VMEM((nz // LANES, 8, LANES), f32),
                pltpu.VMEM((nodes, 8, LANES), f32),
                pltpu.SemaphoreType.REGULAR((2,)),
                dma((13,)),
                dma((3,)),
                dma((3,)),
                dma((2, CHUNKS)),
                dma((2, CHUNKS)),
                dma((2, CHUNKS)),
                dma((2, CHUNKS)),
                dma((2, most)),
                dma((2, most)),
                dma((nodes - 1,)),
                dma((nodes - 1,)),
            ],
            compiler_params=pltpu.CompilerParams(
                collective_id=0, has_side_effects=True, vmem_limit_bytes=56551424
            ),
        )(source, coef, jnp.transpose(flux, (1, 0, 2)), shape, wall)

    return jax.shard_map(
        per_device,
        mesh=mesh,
        in_specs=(
            P("node", None, "slab", None, None),
            P("node", None, "slab", None, None),
            P("node", None, None),
            P("node", None, "slab", None, None),
            P("node", "slab", None),
        ),
        out_specs=P("slab", "node"),
        check_vma=False,
    )
```
